256 devices in a mesh: curve: 128 (over y, z, x_lo, core), chan: 2 (over x_hi).
Axes of the slice: x: 4 (x_hi: 2, x_lo: 2; x = x_hi * 2 + x_lo), y: 4, z: 8, core: 2. Of those that a mesh axis runs over, the one named last changes fastest.
Arguments:
- features: bfloat16 [524288, 256], P('curve', 'chan'), may hold values from -6 to 6
- cotangent: bfloat16 [524288, 256], P('curve', 'chan'), may hold values from -6 to 6
- near_kernel: bfloat16 [4096, 8, 128, 128], P('curve'), may hold values from -0.1875 to 0.1875
- near_index: int32 [4096, 8], P('curve'), may hold values from 0 to 4095, as said below
- near_count: int32 [4096], P('curve'), may hold values from 1 to 8, as said below
- basis_in: bfloat16 [4096, 16, 128], P('curve'), may hold values from -0.09375 to 0.09375
- basis_out: bfloat16 [4096, 128, 16], P('curve'), may hold values from -1.5 to 1.5
- far_kernel: float32 [128, 8, 16, 16], P('curve'), may hold values from -0.5 to 0.5
- far_index: int32 [128, 8], P('curve'), may hold values from 0 to 127, as said below
- channel_mix: float32 [256, 256], replicated, may hold values from -0.375 to 0.375
Outputs:
- layer_out: bfloat16 [524288, 256], P('curve', 'chan')
- feature_grad: bfloat16 [524288, 256], P('curve', 'chan')
The draws below stay inside these ranges and needn't reach their ends.
Inputs may be any that keep to these rules, and one draw needn't show every extreme that they name: `near_index`: slot 0 of block b holds b; every slot of block b holds a block from b - 32 to b. `near_count`: in every group of 32 blocks one block has all 8 slots live and another block has one. `far_index`: every partner of group g differs from g by 2 or more.
All inputs are finite; a program needn't handle non-finite values.
Results may differ from the reference program's by a relative error of at most 0.006.
Values may be sent and summed in bfloat16 or wider, within the bound.
No kernel may reach another device: no remote copies, remote signals or barrier semaphores. Data moves between devices by JAX's collectives and lax.ppermute only.
A program may use at most 128 MiB of HBM per device.

```python
import jax
import jax.numpy as jnp
from jax import lax

P_SIZE = 128
C = 256
R = 16
S = 8
A = 8
NB_DEV = 32
G = 128
NB = 4096
PANELS = 524288


def draw_near_index(key, part):
    block_ids = jnp.arange(NB, dtype=jnp.int32)
    back_steps = jax.random.randint(key, (NB, S), 0, NB_DEV + 1)
    chosen = jnp.maximum(block_ids[:, None] - back_steps, 0)
    slot_ids = jnp.arange(S, dtype=jnp.int32)
    return jnp.where(slot_ids[None, :] == 0, block_ids[:, None], chosen).astype(jnp.int32)


def draw_near_count(key, part):
    key_group = jax.random.fold_in(key, 11)
    key_block = jax.random.fold_in(key, 23)
    key_full = jax.random.fold_in(key, 37)
    key_single = jax.random.fold_in(key, 41)
    ceiling = jax.random.randint(key_group, (G,), 2, S + 1)
    per_block = jnp.repeat(ceiling, NB_DEV)
    raw_count = jax.random.randint(key_block, (NB,), 1, per_block + 1)
    full_pos = jax.random.randint(key_full, (G,), 0, NB_DEV)
    offset = jax.random.randint(key_single, (G,), 1, NB_DEV)
    single_pos = (full_pos + offset) % NB_DEV
    full_rep = jnp.repeat(full_pos, NB_DEV)
    single_rep = jnp.repeat(single_pos, NB_DEV)
    position = jnp.arange(NB, dtype=jnp.int32) % NB_DEV
    shaped = jnp.where(position == single_rep, 1, raw_count)
    return jnp.where(position == full_rep, S, shaped).astype(jnp.int32)


def draw_far_index(key, part):
    offsets = jax.random.randint(key, (G, A), 2, G - 1)
    group_ids = jnp.arange(G, dtype=jnp.int32)[:, None]
    partners = (group_ids + offsets) % G
    slot_ids = jnp.arange(A, dtype=jnp.int32)[None, :]
    partners = jnp.where((group_ids == 0) & (slot_ids == 0), G - 1, partners)
    partners = jnp.where((group_ids == G - 1) & (slot_ids == 0), 0, partners)
    return partners.astype(jnp.int32)


def block_levels(own_key, shape, shards, low, high):
    gain = 1.0
    for dim, parts in shards:
        draws = jax.random.uniform(jax.random.fold_in(jax.random.fold_in(own_key, 6), dim), (parts,), jnp.float32, low / len(shards), high / len(shards))
        gain = gain * jnp.repeat(jnp.exp(draws), shape[dim] // parts).reshape((-1,) + (1,) * (len(shape) - 1 - dim))
    return gain


def bell_draw(key, dims, scale, limit, pieces=(), kind=jnp.bfloat16):
    array = scale * jax.random.normal(key, dims, jnp.float32)
    if pieces:
        array = array * block_levels(key, dims, pieces, -0.22, 0.18)
    return jnp.clip(array, -limit, limit).astype(kind)


def setup_inputs(seed: int = 0) -> dict:
    arg_keys = jax.random.split(jax.random.key(seed), 11)
    return {
        "features": bell_draw(arg_keys[0], (PANELS, C), 1.0, 6.0, ((0, 128), (1, 2))),
        "cotangent": bell_draw(arg_keys[1], (PANELS, C), 1.0, 6.0, ((0, 128), (1, 2))),
        "near_kernel": bell_draw(arg_keys[2], (NB, S, P_SIZE, P_SIZE), (P_SIZE * S) ** -0.5, 0.1875, ((0, 128),)),
        "near_index": draw_near_index(jax.random.fold_in(arg_keys[10], 71), 0),
        "near_count": draw_near_count(jax.random.fold_in(arg_keys[10], 71), 0),
        "basis_in": bell_draw(arg_keys[5], (NB, R, P_SIZE), (P_SIZE * NB_DEV) ** -0.5, 0.09375, ((0, 128),)),
        "basis_out": bell_draw(arg_keys[6], (NB, P_SIZE, R), R ** -0.5, 1.5, ((0, 128),)),
        "far_kernel": bell_draw(arg_keys[7], (G, A, R, R), (R * A) ** -0.5, 0.5, ((0, 128),), jnp.float32),
        "far_index": draw_far_index(jax.random.fold_in(arg_keys[10], 71), 0),
        "channel_mix": bell_draw(arg_keys[9], (C, C), C ** -0.5, 0.375, (), jnp.float32),
    }


def reference(features, cotangent, near_kernel, near_index, near_count, basis_in, basis_out, far_kernel, far_index, channel_mix):
    exact = lax.Precision.HIGHEST
    feat_blocks = features.reshape(NB, P_SIZE, C)
    cot_blocks = cotangent.reshape(NB, P_SIZE, C)
    live_slot = (jnp.arange(S, dtype=jnp.int32)[None, :] < near_count[:, None]).astype(jnp.float32)

    def group_coef(group):
        first_row = (group * NB_DEV).astype(jnp.int32)
        basis_src = lax.dynamic_slice_in_dim(basis_in, first_row, NB_DEV, 0).astype(jnp.float32)
        basis_dst = lax.dynamic_slice_in_dim(basis_out, first_row, NB_DEV, 0).astype(jnp.float32)
        feat_here = lax.dynamic_slice_in_dim(feat_blocks, first_row, NB_DEV, 0).astype(jnp.float32)
        cot_here = lax.dynamic_slice_in_dim(cot_blocks, first_row, NB_DEV, 0).astype(jnp.float32)
        coef = jnp.einsum('brp,bpc->rc', basis_src, feat_here)
        back = jnp.einsum('bpr,bpc->rc', basis_dst, cot_here)
        return coef, back

    coef_all, dfar = lax.map(group_coef, jnp.arange(G, dtype=jnp.int32))
    coarse = coef_all.astype(jnp.bfloat16)
    mixed = jnp.einsum('grc,ck->grk', coarse.astype(jnp.float32), channel_mix, precision=exact)
    far_coef = jnp.einsum('gaqr,garc->gqc', far_kernel, mixed[far_index], precision=exact).astype(jnp.bfloat16)
    spread = jnp.einsum('gaqr,gqc->garc', far_kernel, dfar, precision=exact)
    dmixed = jax.ops.segment_sum(spread.reshape(G * A, R, C), far_index.reshape(G * A), num_segments=G)
    dcoarse = jnp.einsum('grk,ck->grc', dmixed, channel_mix, precision=exact).astype(jnp.bfloat16)

    def group_near(group):
        first_row = (group * NB_DEV).astype(jnp.int32)
        tiles = lax.dynamic_slice_in_dim(near_kernel, first_row, NB_DEV, 0).astype(jnp.float32)
        slot_rows = lax.dynamic_slice_in_dim(near_index, first_row, NB_DEV, 0)
        slot_live = lax.dynamic_slice_in_dim(live_slot, first_row, NB_DEV, 0)
        picked = feat_blocks[slot_rows].astype(jnp.float32) * slot_live[:, :, None, None]
        near = jnp.einsum('bspq,bsqc->bpc', tiles, picked)
        basis_dst = lax.dynamic_slice_in_dim(basis_out, first_row, NB_DEV, 0).astype(jnp.float32)
        far_here = lax.dynamic_index_in_dim(far_coef, group, 0, keepdims=False).astype(jnp.float32)
        layer = near + jnp.einsum('bpr,rc->bpc', basis_dst, far_here)
        cot_here = lax.dynamic_slice_in_dim(cot_blocks, first_row, NB_DEV, 0).astype(jnp.float32)
        contrib = jnp.einsum('bspq,bpc->bsqc', tiles, cot_here) * slot_live[:, :, None, None]
        local_rows = slot_rows - (first_row - NB_DEV)
        one_hot = (local_rows[:, :, None] == jnp.arange(2 * NB_DEV, dtype=jnp.int32)[None, None, :]).astype(jnp.float32)
        extended = jnp.einsum('bse,bsqc->eqc', one_hot, contrib)
        return layer.astype(jnp.bfloat16), extended

    layer_all, extended = lax.map(group_near, jnp.arange(G, dtype=jnp.int32))
    own_part = extended[:, NB_DEV:]
    left_part = extended[:, :NB_DEV]
    moved = jnp.concatenate([left_part[1:], jnp.zeros_like(left_part[:1])], axis=0)
    nearback = (own_part + moved).reshape(NB, P_SIZE, C)
    dcoarse_rep = jnp.repeat(dcoarse, NB_DEV, axis=0).astype(jnp.float32)
    grad = nearback + jnp.einsum('brp,brc->bpc', basis_in.astype(jnp.float32), dcoarse_rep)
    return layer_all.reshape(PANELS, C), grad.astype(jnp.bfloat16).reshape(PANELS, C)
```

```python
import jax
import jax.numpy as jnp
from jax import lax
from jax.experimental import pallas as pl
from jax.experimental.pallas import tpu as pltpu
from jax.sharding import PartitionSpec as P


F32 = jnp.float32
BF16 = jnp.bfloat16
MIB = 1 << 20
QUAD = 4


def params(mib, semantics=("arbitrary",)):
    return pltpu.CompilerParams(dimension_semantics=semantics, vmem_limit_bytes=mib * MIB)


def whole(shape):
    return pl.BlockSpec(shape, lambda *_: (0,) * len(shape))


def dot(a, b, dims=(((1,), (0,)), ((), ()))):
    return lax.dot_general(a, b, dims, preferred_element_type=F32)


def split(value):
    high = value.astype(BF16)
    return high, (value - high.astype(F32)).astype(BF16)


def hbm(value):
    return pltpu.with_memory_space_constraint(value, pltpu.HBM)


def lanes(shape):
    return lax.broadcasted_iota(jnp.int32, shape, 1)


def moved(value, block, keep):
    rolled = pltpu.roll(value, lax.rem(block * 32 + 256, 128), 1)
    return jnp.where(lanes(value.shape) // 32 == keep, rolled, 0.0)


def project_kernel(far_index, feat, cot, b_in, b_out, mix, far, keep, give, pack, acc_f, acc_b):
    step = pl.program_id(0)

    @pl.when(step == 0)
    def _():
        acc_f[...] = jnp.zeros_like(acc_f)
        acc_b[...] = jnp.zeros_like(acc_b)
        wide = jnp.concatenate([far[...], jnp.zeros((128, 112), F32)], axis=1)
        pack[0:16, :] = wide.T[0:16]
        lane = lanes((8, 128)) // 16
        row = jnp.zeros((8, 128), jnp.int32)
        for a in range(8):
            row = jnp.where(lane == a, far_index[0, a], row)
        pack[16:24, :] = row.astype(F32)

    count = b_in.shape[0]
    acc_f[...] += dot(jnp.concatenate([b_in[i] for i in range(count)], axis=1), feat[...])
    acc_b[...] += dot(jnp.concatenate([b_out[i] for i in range(count)], axis=1), cot[...])

    @pl.when(step == pl.num_programs(0) - 1)
    def _():
        half = lax.axis_index("chan")
        start = pl.multiple_of(half * 128, 128)
        exact = lax.Precision.HIGHEST
        coarse = acc_f[...].astype(BF16).astype(F32)
        for oh, out in enumerate((keep, give)):
            there = pl.multiple_of((half ^ oh) * 128, 128)
            out[0:16, :] = jnp.dot(
                coarse,
                mix[pl.ds(start, 128), pl.ds(there, 128)],
                precision=exact,
                preferred_element_type=F32,
            )
            out[16:32, :] = lax.dot_general(
                acc_b[...],
                mix[pl.ds(there, 128), pl.ds(start, 128)],
                (((1,), (1,)), ((), ())),
                precision=exact,
                preferred_element_type=F32,
            )


def deal_kernel(keep, got, pack, *outs):
    me = lax.rem(lax.axis_index("curve"), QUAD)
    both = keep[...] + got[...]
    for os in range(4):
        outs[os][0:32, :] = moved(both, me - (me ^ os), me)
        outs[os][32:56, :] = pack[...]


def backward_kernel(index, count, near, cot, prev, own, acc):
    step = pl.program_id(0)
    per = near.shape[0]
    base = (lax.axis_index("curve") - 1) * 32

    @pl.when(step == 0)
    def _():
        acc[...] = jnp.zeros_like(acc)

    for i in range(per):
        b = step * per + i
        cot_t = cot[i * 128 : (i + 1) * 128, :].T
        live = count[b]
        for k in range(0, 8, 2):
            pair = jnp.concatenate([near[i, k], near[i, k + 1]], axis=1)
            term = dot(cot_t, pair)
            for j in range(2):
                row = jnp.where(k + j < live, index[k + j, b] - base, 64)
                acc[row] += term[:, j * 128 : (j + 1) * 128]

    @pl.when(step == pl.num_programs(0) - 1)
    def _():
        prev[...] = acc[0:32].astype(BF16)
        own[...] = acc[32:64]


def forward_kernel(index, count, near, halo, feat, out, rows):
    step = pl.program_id(0)
    per = near.shape[0]
    base = (lax.axis_index("curve") - 1) * 32

    @pl.when(step == 0)
    def _():
        rows[0:32] = halo[...]
        rows[32:64] = feat[...]
        rows[64] = jnp.zeros((128, 128), BF16)

    for i in range(per):
        b = step * per + i
        live = count[b]
        picked = [
            rows[jnp.where(k < live, index[k, b] - base, 64)] for k in range(8)
        ]
        tiles = jnp.concatenate([near[i, k] for k in range(8)], axis=1)
        out[i * 128 : (i + 1) * 128, :] = dot(tiles, jnp.concatenate(picked, axis=0))


def spread_kernel(*refs):
    msgs, (out, couple), (total,) = refs[:4], refs[4:6], refs[6:]
    me = lax.rem(lax.axis_index("curve"), QUAD)
    value = msgs[0][0:32, :]
    for ref in msgs[1:]:
        value = value + ref[0:32, :]
    fwd = value[0:16].astype(BF16)
    bwd = value[16:32]
    lane = lanes((24, 128))
    for os in range(4):
        total[me ^ os] = msgs[os][32:56, :]
    packed = []
    for a in range(8):
        group = jnp.zeros((24, 128), F32)
        for g in range(4):
            rolled = pltpu.roll(total[g], (16 * (g - a)) % 128, 1)
            group = jnp.where(lane // 16 == g, rolled, group)
        packed.append(group + pltpu.roll(group, 64, 1))
    lane8 = lanes((8, 128))
    for p in range(2):
        quarter = ((lane8 // 16) % 4 + lane8 // 64 + 2 * p) % 4
        wants = [packed[a][16:24].astype(jnp.int32) - quarter for a in range(8)]
        for t in range(32):
            tile = jnp.zeros((16, 128), F32)
            for a in range(8):
                hit = wants[a] == 4 * t
                hit = jnp.concatenate([hit, hit], axis=0)
                tile = tile + jnp.where(hit, packed[a][0:16], 0.0)
            couple[p, t * 16 : (t + 1) * 16, :] = tile
    lane16 = lanes((16, 128))
    block = jnp.concatenate(
        [jnp.where(lane16 // 32 == g, bwd, 0.0) for g in range(4)], axis=0
    )
    contrib = jnp.zeros((512, 128), F32)
    for p in range(2):
        rhs = jnp.concatenate(
            [block if d == 0 else pltpu.roll(block, 32 * d, 1) for d in (2 * p, 2 * p + 1)],
            axis=0,
        )
        r_hi, r_lo = split(rhs)
        k_hi, k_lo = split(couple[p])
        contrib = contrib + (dot(k_hi, r_lo) + dot(k_lo, r_hi)) + dot(k_hi, r_hi)
    contrib = contrib.astype(BF16)
    for t in range(32):
        out[t, 0:16, :] = fwd
        out[t, 16:32, :] = contrib[t * 16 : (t + 1) * 16]


def collect_kernel(arrived, couple, *refs):
    outs, (picked, summed) = refs[:4], refs[4:]
    me = lax.rem(lax.axis_index("curve"), QUAD)
    total = arrived[0, 16:32, :].astype(F32)
    for t in range(1, 32):
        total = total + arrived[t, 16:32, :].astype(F32)
    source = jnp.concatenate([arrived[t, 0:16, :] for t in range(32)], axis=0)
    over_rows = (((0,), (0,)), ((), ()))
    for p in range(2):
        k_hi, k_lo = split(couple[p])
        picked[p * 128 : (p + 1) * 128, :] = dot(k_hi, source, over_rows) + dot(
            k_lo, source, over_rows
        )
    for os in range(4):
        owner = me ^ os
        far = jnp.zeros((16, 128), F32)
        for d in range(4):
            rows = picked[pl.ds(pl.multiple_of(d * 64 + owner * 16, 16), 16), :]
            far = far + moved(rows, me - owner - d, me)
        outs[os][0:16, :] = far.astype(BF16)
        outs[os][16:32, :] = moved(total, me - owner, me).astype(BF16)


def finish_kernel(near, own, arrived, b_in, b_out, m0, m1, m2, m3, layer, grad):
    value = ((m0[...] + m1[...]) + (m2[...] + m3[...])).astype(BF16)
    far = value[0:16]
    coarse_t = value[16:32].astype(F32).T.astype(BF16)
    for i in range(b_in.shape[0]):
        rows = slice(i * 128, (i + 1) * 128)
        term = dot(b_out[i], far, (((0,), (0,)), ((), ())))
        layer[rows, :] = (near[rows, :] + term).astype(BF16)
        total = own[i] + arrived[i].astype(F32) + dot(coarse_t, b_in[i])
        grad[rows, :] = total.astype(BF16).T


def layer_step(
    features,
    cotangent,
    near_kernel,
    near_index,
    near_count,
    basis_in,
    basis_out,
    far_kernel,
    far_index,
    channel_mix,
):
    groups = lax.axis_size("curve")
    blocks = near_kernel.shape[0]
    places = groups // QUAD
    per = 4
    steps = blocks // per
    index = near_index.T
    cube = (blocks, 128, 128)

    halo = lax.ppermute(features, "curve", [(i, i + 1) for i in range(groups - 1)])

    a_steps = 4
    a_blocks = blocks // a_steps
    strip_a = pl.BlockSpec((a_blocks * 128, 128), lambda i: (i, 0))
    thin_a = pl.BlockSpec((a_blocks, 16, 128), lambda i: (i, 0, 0))
    rows32 = jax.ShapeDtypeStruct((32, 128), F32)
    keep, give, pack = pl.pallas_call(
        project_kernel,
        out_shape=[rows32, rows32, jax.ShapeDtypeStruct((24, 128), F32)],
        grid=(a_steps,),
        in_specs=[
            pl.BlockSpec(memory_space=pltpu.SMEM),
            strip_a,
            strip_a,
            thin_a,
            thin_a,
            whole((256, 256)),
            whole((128, 16)),
        ],
        out_specs=[whole((32, 128)), whole((32, 128)), whole((24, 128))],
        scratch_shapes=[pltpu.VMEM((16, 128), F32)] * 2,
        compiler_params=params(40),
        name="project",
    )(
        far_index,
        hbm(features),
        hbm(cotangent),
        hbm(basis_in),
        hbm(jnp.swapaxes(basis_out, 1, 2)),
        hbm(channel_mix),
        hbm(far_kernel.reshape(128, 16)),
    )
    got = lax.ppermute(give, "chan", [(0, 1), (1, 0)])
    msgs = pl.pallas_call(
        deal_kernel,
        out_shape=[jax.ShapeDtypeStruct((56, 128), F32)] * 4,
        compiler_params=params(8, None),
        name="deal",
    )(keep, got, pack)
    seen = [msgs[0]]
    for o in range(1, 4):
        seen.append(lax.ppermute(msgs[o], "curve", [(i, i ^ o) for i in range(groups)]))

    tiles = pl.BlockSpec((per, 8, 128, 128), lambda i, *_: (i, 0, 0, 0))
    strip = pl.BlockSpec((per * 128, 128), lambda i, *_: (i, 0))
    prev, own = pl.pallas_call(
        backward_kernel,
        out_shape=[jax.ShapeDtypeStruct(cube, BF16), jax.ShapeDtypeStruct(cube, F32)],
        grid_spec=pltpu.PrefetchScalarGridSpec(
            num_scalar_prefetch=2,
            grid=(steps,),
            in_specs=[tiles, strip],
            out_specs=[whole(cube), whole(cube)],
            scratch_shapes=[pltpu.VMEM((65, 128, 128), F32)],
        ),
        compiler_params=params(40),
        cost_estimate=pl.CostEstimate(flops=8 << 30, bytes_accessed=12 << 20, transcendentals=0),
        name="backward",
    )(index, near_count, hbm(near_kernel), hbm(cotangent))
    arrived = lax.ppermute(prev, "curve", [(i + 1, i) for i in range(groups - 1)])

    out_msg, couple = pl.pallas_call(
        spread_kernel,
        out_shape=[
            pltpu.HBM((places, 32, 128), BF16),
            pltpu.HBM((2, places * 16, 128), F32),
        ],
        scratch_shapes=[pltpu.VMEM((4, 24, 128), F32)],
        compiler_params=params(8, None),
        name="spread",
    )(*seen)
    rings = [[t * QUAD + s for t in range(places)] for s in range(QUAD)]
    in_msg = lax.all_to_all(out_msg, "curve", 0, 0, tiled=True, axis_index_groups=rings)

    near = pl.pallas_call(
        forward_kernel,
        out_shape=pltpu.HBM((blocks * 128, 128), F32),
        grid_spec=pltpu.PrefetchScalarGridSpec(
            num_scalar_prefetch=2,
            grid=(steps,),
            in_specs=[tiles, whole(cube), whole(cube)],
            out_specs=strip,
            scratch_shapes=[pltpu.VMEM((65, 128, 128), BF16)],
        ),
        compiler_params=params(40),
        cost_estimate=pl.CostEstimate(flops=8 << 30, bytes_accessed=12 << 20, transcendentals=0),
        name="forward",
    )(index, near_count, hbm(near_kernel), halo.reshape(cube), hbm(features.reshape(cube)))

    back = pl.pallas_call(
        collect_kernel,
        out_shape=[jax.ShapeDtypeStruct((32, 128), BF16)] * 4,
        scratch_shapes=[pltpu.VMEM((256, 128), F32), pltpu.VMEM((16, 128), F32)],
        compiler_params=params(8, None),
        name="collect",
    )(in_msg, hbm(couple))
    home = [back[0]]
    for o in range(1, 4):
        home.append(lax.ppermute(back[o], "curve", [(i, i ^ o) for i in range(groups)]))

    block3 = pl.BlockSpec((per, 128, 128), lambda i: (i, 0, 0))
    thin = pl.BlockSpec((per, 16, 128), lambda i: (i, 0, 0))
    strip1 = pl.BlockSpec((per * 128, 128), lambda i: (i, 0))
    layer, grad = pl.pallas_call(
        finish_kernel,
        out_shape=[jax.ShapeDtypeStruct((blocks * 128, 128), BF16)] * 2,
        grid=(steps,),
        in_specs=[strip1, block3, block3, thin, thin] + [whole((32, 128))] * 4,
        out_specs=[strip1, strip1],
        compiler_params=params(40),
        name="finish",
    )(
        hbm(near), own, arrived, hbm(basis_in), hbm(jnp.swapaxes(basis_out, 1, 2)), *home
    )
    return (layer, grad)


def solution(mesh):
    return jax.shard_map(
        layer_step,
        mesh=mesh,
        in_specs=(
            P("curve", "chan"),
            P("curve", "chan"),
            P("curve", None, None, None),
            P("curve", None),
            P("curve"),
            P("curve", None, None),
            P("curve", None, None),
            P("curve", None, None, None),
            P("curve", None),
            P(),
        ),
        out_specs=(P("curve", "chan"), P("curve", "chan")),
        check_vma=False,
    )
```

```python
import jax
import jax.numpy as jnp
from jax import lax
from jax.experimental import pallas as pl
from jax.experimental.pallas import tpu as pltpu
from jax.sharding import PartitionSpec as P


F32 = jnp.float32
BF16 = jnp.bfloat16
MIB = 1 << 20
QUAD = 4
ZS = 8
PARTS = 4
UNROLL = 4


def params(mib, semantics=("arbitrary",)):
    return pltpu.CompilerParams(dimension_semantics=semantics, vmem_limit_bytes=mib * MIB)


def dot(a, b, dims=(((1,), (0,)), ((), ()))):
    return lax.dot_general(a, b, dims, preferred_element_type=F32)


def split(value):
    high = value.astype(BF16)
    return high, (value - high.astype(F32)).astype(BF16)


def hbm(value):
    return pltpu.with_memory_space_constraint(value, pltpu.HBM)


def lanes(shape):
    return lax.broadcasted_iota(jnp.int32, shape, 1)


def moved(value, block, keep):
    rolled = pltpu.roll(value, lax.rem(block * 32 + 256, 128), 1)
    return jnp.where(lanes(value.shape) // 32 == keep, rolled, 0.0)


def project_kernel(
    far_index, feat, cot, near, b_in, b_out, mix, far,
    keep, give, pack, feat_v, cot_v, near_v,
    b_in_v, b_out_v, mix_v, far_v, sems,
):
    count = feat.shape[0]
    part = count // PARTS
    loads = []
    for n in range(PARTS):
        rows = pl.ds(n * part, part)
        loads.append(
            [
                pltpu.make_async_copy(src.at[rows], dst.at[rows], sems.at[n, j])
                for j, (src, dst) in enumerate(
                    ((feat, feat_v), (b_in, b_in_v), (cot, cot_v), (b_out, b_out_v))
                )
            ]
        )
    small = [
        pltpu.make_async_copy(mix, mix_v, sems.at[PARTS, 0]),
        pltpu.make_async_copy(far, far_v, sems.at[PARTS, 1]),
    ]
    big = [
        pltpu.make_async_copy(near.at[pl.ds(n * part, part)], near_v.at[pl.ds(n * part, part)], sems.at[n, 4])
        for n in range(PARTS)
    ]
    for copy in [c for group in loads for c in group] + small + big:
        copy.start()

    acc_f = jnp.zeros((16, 128), F32)
    acc_b = jnp.zeros((16, 128), F32)
    for n in range(PARTS):
        for copy in loads[n]:
            copy.wait()
        picks = range(n * part, (n + 1) * part)
        acc_f += dot(
            jnp.concatenate([b_in_v[i] for i in picks], axis=1),
            feat_v[n * part : (n + 1) * part].reshape(part * 128, 128),
        )
        acc_b += dot(
            jnp.concatenate([b_out_v[i] for i in picks], axis=1),
            cot_v[n * part : (n + 1) * part].reshape(part * 128, 128),
        )
    for copy in small:
        copy.wait()
    half = lax.axis_index("chan")
    start = pl.multiple_of(half * 128, 128)
    exact = lax.Precision.HIGHEST
    coarse = acc_f.astype(BF16).astype(F32)
    for oh, out in enumerate((keep, give)):
        there = pl.multiple_of((half ^ oh) * 128, 128)
        out[0:16, :] = jnp.dot(
            coarse,
            mix_v[pl.ds(start, 128), pl.ds(there, 128)],
            precision=exact,
            preferred_element_type=F32,
        )
        out[16:32, :] = lax.dot_general(
            acc_b,
            mix_v[pl.ds(there, 128), pl.ds(start, 128)],
            (((1,), (1,)), ((), ())),
            precision=exact,
            preferred_element_type=F32,
        )
    wide = jnp.concatenate([far_v[...], jnp.zeros((128, 112), F32)], axis=1)
    pack[0:16, :] = wide.T[0:16]
    lane = lanes((8, 128)) // 16
    row = jnp.zeros((8, 128), jnp.int32)
    for a in range(8):
        row = jnp.where(lane == a, far_index[0, a], row)
    pack[16:24, :] = row.astype(F32)
    for copy in big:
        copy.wait()


def deal_kernel(keep, got, pack, *outs):
    me = lax.rem(lax.axis_index("curve"), QUAD)
    both = keep[...] + got[...]
    for os in range(4):
        outs[os][0:32, :] = moved(both, me - (me ^ os), me)
        outs[os][32:56, :] = pack[...]


def backward_kernel(index, count, near, cot, prev, acc):
    base = (lax.axis_index("curve") - 1) * 32
    acc[...] = jnp.zeros_like(acc)

    def some(step, carry):
        for i in range(UNROLL):
            b = step * UNROLL + i
            cot_t = cot[b].T
            live = count[b]
            for k in range(0, 8, 2):
                pair = jnp.concatenate([near[b, k], near[b, k + 1]], axis=1)
                term = dot(cot_t, pair)
                for j in range(2):
                    row = jnp.where(k + j < live, index[k + j, b] - base, 64)
                    acc[row] += term[:, j * 128 : (j + 1) * 128]
        return carry

    lax.fori_loop(0, near.shape[0] // UNROLL, some, 0)
    prev[...] = acc[0:32].astype(BF16)


def forward_kernel(first, index, count, near, rows, out):
    base = (lax.axis_index("curve") - 1) * 32

    def some(step, carry):
        for i in range(UNROLL):
            n = step * UNROLL + i
            b = first + n
            live = count[b]
            picked = [rows[jnp.where(k < live, index[k, b] - base, 64)] for k in range(8)]
            tiles = jnp.concatenate([near[b, k] for k in range(8)], axis=1)
            out[n] = dot(tiles, jnp.concatenate(picked, axis=0))
        return carry

    lax.fori_loop(0, out.shape[0] // UNROLL, some, 0)


def forward_a_kernel(index, count, near, halo, feat, rows, out):
    rows[0:32] = halo[...]
    rows[32:64] = feat[...]
    rows[64] = jnp.zeros((128, 128), BF16)
    forward_kernel(0, index, count, near, rows, out)


def forward_b_kernel(index, count, near, rows, out):
    forward_kernel(out.shape[0], index, count, near, rows, out)


def place():
    t = lax.axis_index("curve") // QUAD
    return t // ZS, lax.rem(t, ZS)


def spread_kernel(*refs):
    msgs, outs, couple, total, held = refs[:4], refs[4:8], refs[8], refs[9], refs[10]
    me = lax.rem(lax.axis_index("curve"), QUAD)
    value = msgs[0][0:32, :]
    for ref in msgs[1:]:
        value = value + ref[0:32, :]
    fwd = value[0:16].astype(BF16)
    bwd = value[16:32]
    lane = lanes((24, 128))
    for os in range(4):
        total[me ^ os] = msgs[os][32:56, :]
    packed = []
    for a in range(8):
        group = jnp.zeros((24, 128), F32)
        for g in range(4):
            rolled = pltpu.roll(total[g], (16 * (g - a)) % 128, 1)
            group = jnp.where(lane // 16 == g, rolled, group)
        packed.append(group + pltpu.roll(group, 64, 1))
    lane8 = lanes((8, 128))
    for p in range(2):
        quarter = ((lane8 // 16) % 4 + lane8 // 64 + 2 * p) % 4
        wants = [packed[a][16:24].astype(jnp.int32) - quarter for a in range(8)]
        for t in range(32):
            tile = jnp.zeros((16, 128), F32)
            for a in range(8):
                hit = wants[a] == 4 * t
                hit = jnp.concatenate([hit, hit], axis=0)
                tile = tile + jnp.where(hit, packed[a][0:16], 0.0)
            couple[p, t * 16 : (t + 1) * 16, :] = tile
    lane16 = lanes((16, 128))
    block = jnp.concatenate(
        [jnp.where(lane16 // 32 == g, bwd, 0.0) for g in range(4)], axis=0
    )
    contrib = jnp.zeros((512, 128), F32)
    for p in range(2):
        rhs = jnp.concatenate(
            [block if d == 0 else pltpu.roll(block, 32 * d, 1) for d in (2 * p, 2 * p + 1)],
            axis=0,
        )
        r_hi, r_lo = split(rhs)
        k_hi, k_lo = split(couple[p])
        contrib = contrib + (dot(k_hi, r_lo) + dot(k_lo, r_hi)) + dot(k_hi, r_hi)
    held[...] = contrib.astype(BF16)
    y, _ = place()
    for oy in range(4):
        first = pl.multiple_of((y ^ oy) * (ZS * 16), ZS * 16)
        outs[oy][0:16, :] = fwd
        outs[oy][16:144, :] = held[pl.ds(first, ZS * 16), :]


def block16(n):
    return pl.ds(pl.multiple_of(n * 16, 16), 16)


def along_kernel(r0, r1, r2, r3, up, down, mine, held):
    _, z = place()
    seen = (r0, r1, r2, r3)
    total = r0[16:144, :].astype(F32)
    for ref in seen[1:]:
        total = total + ref[16:144, :].astype(F32)
    held[...] = total
    for oy in range(4):
        piece = seen[oy][0:16, :]
        for out in (up, down, mine):
            out[oy * 16 : oy * 16 + 16, :] = piece

    def target(d):
        return held[block16(lax.rem(z + d + ZS, ZS)), :].astype(BF16)

    for n, d in enumerate((2, 3, 4)):
        up[64 + n * 16 : 80 + n * 16, :] = target(d)
    for n, d in enumerate((-3, -2)):
        down[64 + n * 16 : 80 + n * 16, :] = target(d)
    for n, d in enumerate((-1, 0, 1)):
        mine[64 + n * 16 : 80 + n * 16, :] = target(d)


def beside_kernel(mine, low, high, up, down, kept):
    def part(ref, n):
        return ref[64 + n * 16 : 80 + n * 16, :].astype(F32)

    before = part(mine, 0) + part(low, 0)
    here = part(mine, 1) + part(low, 1) + part(high, 0)
    after = part(mine, 2) + part(low, 2) + part(high, 1)
    up[0:64, :] = mine[0:64, :]
    up[64:128, :] = low[0:64, :]
    up[128:192, :] = high[0:64, :]
    up[192:208, :] = after.astype(BF16)
    down[0:64, :] = mine[0:64, :]
    down[64:128, :] = low[0:64, :]
    down[128:144, :] = before.astype(BF16)
    kept[...] = here


def collect_kernel(mine, low, high, prior, later, kept, couple, *refs):
    outs, (picked, source) = refs[:4], refs[4:]
    me = lax.rem(lax.axis_index("curve"), QUAD)
    y, z = place()
    total = kept[...] + prior[192:208, :].astype(F32) + later[128:144, :].astype(F32)
    held = (
        (mine, 0, 0), (low, 0, -3), (high, 0, 3),
        (prior, 0, -1), (prior, 64, -4), (prior, 128, 2),
        (later, 0, 1), (later, 64, -2),
    )
    for ref, first, d in held:
        column = lax.rem(z + d + ZS, ZS)
        for oy in range(4):
            rows = slice(first + oy * 16, first + oy * 16 + 16)
            source[block16((y ^ oy) * ZS + column), :] = ref[rows, :]
    whole_source = source[...]
    over_rows = (((0,), (0,)), ((), ()))
    for p in range(2):
        k_hi, k_lo = split(couple[p])
        picked[p * 128 : (p + 1) * 128, :] = dot(k_hi, whole_source, over_rows) + dot(
            k_lo, whole_source, over_rows
        )
    for os in range(4):
        owner = me ^ os
        far = jnp.zeros((16, 128), F32)
        for d in range(4):
            rows = picked[pl.ds(pl.multiple_of(d * 64 + owner * 16, 16), 16), :]
            far = far + moved(rows, me - owner - d, me)
        outs[os][0:16, :] = far.astype(BF16)
        outs[os][16:32, :] = moved(total, me - owner, me).astype(BF16)


def finish_kernel(
    near_a, near_b, acc, arrived, b_in, b_out, m0, m1, m2, m3, layer, grad, layer_v, grad_v, sems
):
    value = ((m0[...] + m1[...]) + (m2[...] + m3[...])).astype(BF16)
    far = value[0:16]
    coarse_t = value[16:32].astype(F32).T.astype(BF16)
    copies = []
    cut = near_a.shape[0]
    part = 2 * cut // PARTS
    for n in range(PARTS):
        for i in range(n * part, (n + 1) * part):
            near = near_a[i] if i < cut else near_b[i - cut]
            term = dot(b_out[i], far, (((0,), (0,)), ((), ())))
            layer_v[i] = (near + term).astype(BF16)
            total = acc[32 + i] + arrived[i].astype(F32) + dot(coarse_t, b_in[i])
            grad_v[i] = total.astype(BF16).T
        for j, (src, dst) in enumerate(((layer_v, layer), (grad_v, grad))):
            rows = pl.ds(n * part, part)
            copies.append(pltpu.make_async_copy(src.at[rows], dst.at[rows], sems.at[n, j]))
            copies[-1].start()
    for copy in copies:
        copy.wait()


def layer_step(
    features,
    cotangent,
    near_kernel,
    near_index,
    near_count,
    basis_in,
    basis_out,
    far_kernel,
    far_index,
    channel_mix,
):
    groups = lax.axis_size("curve")
    blocks = near_kernel.shape[0]
    places = groups // QUAD
    index = near_index.T
    cube = (blocks, 128, 128)

    halo = lax.ppermute(features, "curve", [(i, i + 1) for i in range(groups - 1)])

    b_out = jnp.swapaxes(basis_out, 1, 2)
    rows32 = jax.ShapeDtypeStruct((32, 128), F32)
    vmem = pl.BlockSpec(memory_space=pltpu.VMEM)
    smem = pl.BlockSpec(memory_space=pltpu.SMEM)
    raw = pl.BlockSpec(memory_space=pl.ANY)
    keep, give, pack, feat_v, cot_v, near_v = pl.pallas_call(
        project_kernel,
        out_shape=[
            rows32,
            rows32,
            jax.ShapeDtypeStruct((24, 128), F32),
            pltpu.VMEM(cube, BF16),
            pltpu.VMEM(cube, BF16),
            pltpu.VMEM(near_kernel.shape, BF16),
        ],
        in_specs=[smem] + [raw] * 7,
        out_specs=[vmem] * 6,
        scratch_shapes=[
            pltpu.VMEM((blocks, 16, 128), BF16),
            pltpu.VMEM((blocks, 16, 128), BF16),
            pltpu.VMEM((256, 256), F32),
            pltpu.VMEM((128, 16), F32),
            pltpu.SemaphoreType.DMA((PARTS + 1, 5)),
        ],
        compiler_params=params(14, None),
        name="project",
    )(
        far_index,
        hbm(features.reshape(cube)),
        hbm(cotangent.reshape(cube)),
        hbm(near_kernel),
        hbm(basis_in),
        hbm(b_out),
        hbm(channel_mix),
        hbm(far_kernel.reshape(128, 16)),
    )
    got = lax.ppermute(give, "chan", [(0, 1), (1, 0)])
    msgs = pl.pallas_call(
        deal_kernel,
        out_shape=[jax.ShapeDtypeStruct((56, 128), F32)] * 4,
        compiler_params=params(8, None),
        name="deal",
    )(keep, got, pack)
    seen = [msgs[0]]
    for o in range(1, 4):
        seen.append(lax.ppermute(msgs[o], "curve", [(i, i ^ o) for i in range(groups)]))

    prev, acc = pl.pallas_call(
        backward_kernel,
        out_shape=[
            jax.ShapeDtypeStruct(cube, BF16),
            pltpu.VMEM((2 * blocks + 1, 128, 128), F32),
        ],
        in_specs=[smem, smem, vmem, vmem],
        out_specs=[vmem, vmem],
        compiler_params=params(14, None),
        cost_estimate=pl.CostEstimate(flops=8 << 30, bytes_accessed=12 << 20, transcendentals=0),
        name="backward",
    )(index, near_count, near_v, cot_v)
    arrived = lax.ppermute(prev, "curve", [(i + 1, i) for i in range(groups - 1)])

    def bf16_rows(n):
        return jax.ShapeDtypeStruct((n, 128), BF16)

    y0, y1, y2, y3, couple = pl.pallas_call(
        spread_kernel,
        out_shape=[bf16_rows(144)] * 4 + [jax.ShapeDtypeStruct((2, places * 16, 128), F32)],
        scratch_shapes=[pltpu.VMEM((4, 24, 128), F32), pltpu.VMEM((places * 16, 128), BF16)],
        compiler_params=params(6, None),
        name="spread",
    )(*seen)
    ways = [y0]
    for o, sent in ((1, y1), (2, y2), (3, y3)):
        pairs = [(i, i ^ (o * ZS * QUAD)) for i in range(groups)]
        ways.append(lax.ppermute(sent, "curve", pairs))

    half_cube = jax.ShapeDtypeStruct((blocks // 2, 128, 128), F32)
    half_cost = pl.CostEstimate(flops=4 << 30, bytes_accessed=6 << 20, transcendentals=0)
    rows, near_a = pl.pallas_call(
        forward_a_kernel,
        out_shape=[
            pltpu.VMEM((2 * blocks + 1, 128, 128), BF16),
            pltpu.VMEM(half_cube.shape, F32),
        ],
        in_specs=[smem, smem, vmem, vmem, vmem],
        out_specs=[vmem, vmem],
        compiler_params=params(6, None),
        cost_estimate=half_cost,
        name="forward_a",
    )(index, near_count, near_v, halo.reshape(cube), feat_v)

    up3, down3, mine = pl.pallas_call(
        along_kernel,
        out_shape=[bf16_rows(112), bf16_rows(96), bf16_rows(112)],
        scratch_shapes=[pltpu.VMEM((ZS * 16, 128), F32)],
        compiler_params=params(6, None),
        name="along",
    )(*ways)

    def turned(value, shift):
        def at(i):
            z = (i // QUAD) % ZS
            return i + ((z + shift) % ZS - z) * QUAD

        return lax.ppermute(value, "curve", [(i, at(i)) for i in range(groups)])

    low = turned(up3, 3)
    high = turned(down3, -3)
    near_b = pl.pallas_call(
        forward_b_kernel,
        out_shape=pltpu.VMEM(half_cube.shape, F32),
        in_specs=[smem, smem, vmem, vmem],
        out_specs=vmem,
        compiler_params=params(6, None),
        cost_estimate=half_cost,
        name="forward_b",
    )(index, near_count, near_v, rows)

    up1, down1, kept = pl.pallas_call(
        beside_kernel,
        out_shape=[bf16_rows(208), bf16_rows(144), jax.ShapeDtypeStruct((16, 128), F32)],
        compiler_params=params(6, None),
        name="beside",
    )(mine, low, high)
    prior = turned(up1, 1)
    later = turned(down1, -1)

    back = pl.pallas_call(
        collect_kernel,
        out_shape=[bf16_rows(32)] * 4,
        scratch_shapes=[pltpu.VMEM((256, 128), F32), pltpu.VMEM((places * 16, 128), BF16)],
        compiler_params=params(6, None),
        name="collect",
    )(mine, low, high, prior, later, kept, couple)
    home = [back[0]]
    for o in range(1, 4):
        home.append(lax.ppermute(back[o], "curve", [(i, i ^ o) for i in range(groups)]))

    layer, grad = pl.pallas_call(
        finish_kernel,
        out_shape=[pltpu.HBM(cube, BF16)] * 2,
        in_specs=[vmem] * 10,
        out_specs=[raw, raw],
        scratch_shapes=[
            pltpu.VMEM(cube, BF16),
            pltpu.VMEM(cube, BF16),
            pltpu.SemaphoreType.DMA((PARTS, 2)),
        ],
        compiler_params=params(14, None),
        name="finish",
    )(near_a, near_b, acc, arrived, basis_in, b_out, *home)
    return (layer.reshape(features.shape), grad.reshape(features.shape))


def solution(mesh):
    return jax.shard_map(
        layer_step,
        mesh=mesh,
        in_specs=(
            P("curve", "chan"),
            P("curve", "chan"),
            P("curve", None, None, None),
            P("curve", None),
            P("curve"),
            P("curve", None, None),
            P("curve", None, None),
            P("curve", None, None, None),
            P("curve", None),
            P(),
        ),
        out_specs=(P("curve", "chan"), P("curve", "chan")),
        check_vma=False,
    )
```

```python
import jax
import jax.numpy as jnp
from jax import lax
from jax.experimental import pallas as pl
from jax.experimental.pallas import tpu as pltpu
from jax.sharding import PartitionSpec as P


F32 = jnp.float32
BF16 = jnp.bfloat16
MIB = 1 << 20
QUAD = 4
PARTS = 4
CHUNKS = 4
UNROLL = 4


def params(mib, semantics=("arbitrary",)):
    return pltpu.CompilerParams(dimension_semantics=semantics, vmem_limit_bytes=mib * MIB)


def dot(a, b, dims=(((1,), (0,)), ((), ()))):
    return lax.dot_general(a, b, dims, preferred_element_type=F32)


def split(value):
    high = value.astype(BF16)
    return high, (value - high.astype(F32)).astype(BF16)


def hbm(value):
    return pltpu.with_memory_space_constraint(value, pltpu.HBM)


def lanes(shape):
    return lax.broadcasted_iota(jnp.int32, shape, 1)


def moved(value, block, keep):
    rolled = pltpu.roll(value, lax.rem(block * 32 + 256, 128), 1)
    return jnp.where(lanes(value.shape) // 32 == keep, rolled, 0.0)


def project_kernel(feat, cot, b_in, b_out, mix, keep, give, cot_v, feat_v, b_in_v, b_out_v, mix_v, sems):
    count = feat.shape[0]
    part = count // PARTS
    loads = []
    for n in range(PARTS):
        rows = pl.ds(n * part, part)
        loads.append(
            [
                pltpu.make_async_copy(src.at[rows], dst.at[rows], sems.at[n, j])
                for j, (src, dst) in enumerate(
                    ((feat, feat_v), (b_in, b_in_v), (cot, cot_v), (b_out, b_out_v))
                )
            ]
        )
    last = pltpu.make_async_copy(mix, mix_v, sems.at[PARTS, 0])
    for copy in [c for group in loads for c in group] + [last]:
        copy.start()

    acc_f = jnp.zeros((16, 128), F32)
    acc_b = jnp.zeros((16, 128), F32)
    for n in range(PARTS):
        for copy in loads[n]:
            copy.wait()
        picks = range(n * part, (n + 1) * part)
        acc_f += dot(
            jnp.concatenate([b_in_v[i] for i in picks], axis=1),
            feat_v[n * part : (n + 1) * part].reshape(part * 128, 128),
        )
        acc_b += dot(
            jnp.concatenate([b_out_v[i] for i in picks], axis=1),
            cot_v[n * part : (n + 1) * part].reshape(part * 128, 128),
        )
    last.wait()
    half = lax.axis_index("chan")
    start = pl.multiple_of(half * 128, 128)
    exact = lax.Precision.HIGHEST
    coarse = acc_f.astype(BF16).astype(F32)
    for oh, out in enumerate((keep, give)):
        there = pl.multiple_of((half ^ oh) * 128, 128)
        out[0:16, :] = jnp.dot(
            coarse,
            mix_v[pl.ds(start, 128), pl.ds(there, 128)],
            precision=exact,
            preferred_element_type=F32,
        )
        out[16:32, :] = lax.dot_general(
            acc_b,
            mix_v[pl.ds(there, 128), pl.ds(start, 128)],
            (((1,), (1,)), ((), ())),
            precision=exact,
            preferred_element_type=F32,
        )


def deal_kernel(far_index, far, keep, got, *outs):
    me = lax.rem(lax.axis_index("curve"), QUAD)
    both = keep[...] + got[...]
    wide = jnp.concatenate([far[...], jnp.zeros((128, 112), F32)], axis=1)
    pack = wide.T[0:16]
    lane = lanes((8, 128)) // 16
    row = jnp.zeros((8, 128), jnp.int32)
    for a in range(8):
        row = jnp.where(lane == a, far_index[0, a], row)
    for os in range(4):
        outs[os][0:32, :] = moved(both, me - (me ^ os), me)
        outs[os][32:48, :] = pack
        outs[os][48:56, :] = row.astype(F32)


def tile_loads(near, near_v, sems):
    part = near.shape[0] // CHUNKS
    copies = []
    for n in range(CHUNKS):
        rows = pl.ds(n * part, part)
        copies.append(pltpu.make_async_copy(near.at[rows], near_v.at[rows], sems.at[n]))
        copies[-1].start()
    return copies


def backward_kernel(index, count, near, cot, prev, acc, near_v, sems):
    base = (lax.axis_index("curve") - 1) * 32
    copies = tile_loads(near, near_v, sems)
    acc[...] = jnp.zeros_like(acc)
    part = near.shape[0] // CHUNKS
    for n, copy in enumerate(copies):
        copy.wait()

        def some(step, carry):
            for i in range(UNROLL):
                b = n * part + step * UNROLL + i
                cot_t = cot[b].T
                live = count[b]
                for k in range(0, 8, 2):
                    pair = jnp.concatenate([near_v[b, k], near_v[b, k + 1]], axis=1)
                    term = dot(cot_t, pair)
                    for j in range(2):
                        row = jnp.where(k + j < live, index[k + j, b] - base, 64)
                        acc[row] += term[:, j * 128 : (j + 1) * 128]
            return carry

        lax.fori_loop(0, part // UNROLL, some, 0)
    prev[...] = acc[0:32].astype(BF16)


def forward_kernel(index, count, near, halo, feat, out, rows, near_v, out_v, sems, row_sems, out_sems):
    base = (lax.axis_index("curve") - 1) * 32
    heads = [
        pltpu.make_async_copy(feat, rows.at[pl.ds(32, 32)], row_sems.at[0]),
        pltpu.make_async_copy(halo, rows.at[pl.ds(0, 32)], row_sems.at[1]),
    ]
    for copy in heads:
        copy.start()
    copies = tile_loads(near, near_v, sems)
    rows[64] = jnp.zeros((128, 128), BF16)
    for copy in heads:
        copy.wait()
    part = near.shape[0] // CHUNKS
    stores = []
    for n, copy in enumerate(copies):
        copy.wait()

        def some(step, carry):
            for i in range(UNROLL):
                b = n * part + step * UNROLL + i
                live = count[b]
                picked = [rows[jnp.where(k < live, index[k, b] - base, 64)] for k in range(8)]
                tiles = jnp.concatenate([near_v[b, k] for k in range(8)], axis=1)
                out_v[b] = dot(tiles, jnp.concatenate(picked, axis=0))
            return carry

        lax.fori_loop(0, part // UNROLL, some, 0)
        span = pl.ds(n * part, part)
        stores.append(pltpu.make_async_copy(out_v.at[span], out.at[span], out_sems.at[n]))
        stores[-1].start()
    for copy in stores:
        copy.wait()


def spread_kernel(*refs):
    msgs, acc, (out, couple, own), total, sem = refs[:4], refs[4], refs[5:8], refs[8], refs[9]
    saved = pltpu.make_async_copy(acc.at[pl.ds(32, 32)], own, sem)
    saved.start()
    me = lax.rem(lax.axis_index("curve"), QUAD)
    value = msgs[0][0:32, :]
    for ref in msgs[1:]:
        value = value + ref[0:32, :]
    fwd = value[0:16].astype(BF16)
    bwd = value[16:32]
    lane = lanes((24, 128))
    for os in range(4):
        total[me ^ os] = msgs[os][32:56, :]
    packed = []
    for a in range(8):
        group = jnp.zeros((24, 128), F32)
        for g in range(4):
            rolled = pltpu.roll(total[g], (16 * (g - a)) % 128, 1)
            group = jnp.where(lane // 16 == g, rolled, group)
        packed.append(group + pltpu.roll(group, 64, 1))
    lane8 = lanes((8, 128))
    for p in range(2):
        quarter = ((lane8 // 16) % 4 + lane8 // 64 + 2 * p) % 4
        wants = [packed[a][16:24].astype(jnp.int32) - quarter for a in range(8)]
        for t in range(32):
            tile = jnp.zeros((16, 128), F32)
            for a in range(8):
                hit = wants[a] == 4 * t
                hit = jnp.concatenate([hit, hit], axis=0)
                tile = tile + jnp.where(hit, packed[a][0:16], 0.0)
            couple[p, t * 16 : (t + 1) * 16, :] = tile
    lane16 = lanes((16, 128))
    block = jnp.concatenate(
        [jnp.where(lane16 // 32 == g, bwd, 0.0) for g in range(4)], axis=0
    )
    contrib = jnp.zeros((512, 128), F32)
    for p in range(2):
        rhs = jnp.concatenate(
            [block if d == 0 else pltpu.roll(block, 32 * d, 1) for d in (2 * p, 2 * p + 1)],
            axis=0,
        )
        r_hi, r_lo = split(rhs)
        k_hi, k_lo = split(couple[p])
        contrib = contrib + (dot(k_hi, r_lo) + dot(k_lo, r_hi)) + dot(k_hi, r_hi)
    contrib = contrib.astype(BF16)
    for t in range(32):
        out[t, 0:16, :] = fwd
        out[t, 16:32, :] = contrib[t * 16 : (t + 1) * 16]
    saved.wait()


def collect_kernel(arrived, couple, *refs):
    outs, (picked, summed) = refs[:4], refs[4:]
    me = lax.rem(lax.axis_index("curve"), QUAD)
    total = arrived[0, 16:32, :].astype(F32)
    for t in range(1, 32):
        total = total + arrived[t, 16:32, :].astype(F32)
    source = jnp.concatenate([arrived[t, 0:16, :] for t in range(32)], axis=0)
    over_rows = (((0,), (0,)), ((), ()))
    for p in range(2):
        k_hi, k_lo = split(couple[p])
        picked[p * 128 : (p + 1) * 128, :] = dot(k_hi, source, over_rows) + dot(
            k_lo, source, over_rows
        )
    for os in range(4):
        owner = me ^ os
        far = jnp.zeros((16, 128), F32)
        for d in range(4):
            rows = picked[pl.ds(pl.multiple_of(d * 64 + owner * 16, 16), 16), :]
            far = far + moved(rows, me - owner - d, me)
        outs[os][0:16, :] = far.astype(BF16)
        outs[os][16:32, :] = moved(total, me - owner, me).astype(BF16)


def fetch_kernel(near, own, near_v, own_v, sems):
    copies = [
        pltpu.make_async_copy(near, near_v, sems.at[0]),
        pltpu.make_async_copy(own, own_v, sems.at[1]),
    ]
    for copy in copies:
        copy.start()
    for copy in copies:
        copy.wait()


def finish_kernel(
    near, own, arrived, b_in, b_out, m0, m1, m2, m3, layer, grad, layer_v, grad_v, sems
):
    value = ((m0[...] + m1[...]) + (m2[...] + m3[...])).astype(BF16)
    far = value[0:16]
    coarse_t = value[16:32].astype(F32).T.astype(BF16)
    copies = []
    part = near.shape[0] // PARTS
    for n in range(PARTS):
        for i in range(n * part, (n + 1) * part):
            term = dot(b_out[i], far, (((0,), (0,)), ((), ())))
            layer_v[i] = (near[i] + term).astype(BF16)
            total = own[i] + arrived[i].astype(F32) + dot(coarse_t, b_in[i])
            grad_v[i] = total.astype(BF16).T
        for j, (src, dst) in enumerate(((layer_v, layer), (grad_v, grad))):
            rows = pl.ds(n * part, part)
            copies.append(pltpu.make_async_copy(src.at[rows], dst.at[rows], sems.at[n, j]))
            copies[-1].start()
    for copy in copies:
        copy.wait()


def layer_step(
    features,
    cotangent,
    near_kernel,
    near_index,
    near_count,
    basis_in,
    basis_out,
    far_kernel,
    far_index,
    channel_mix,
):
    groups = lax.axis_size("curve")
    blocks = near_kernel.shape[0]
    places = groups // QUAD
    index = near_index.T
    cube = (blocks, 128, 128)

    halo = lax.ppermute(features, "curve", [(i, i + 1) for i in range(groups - 1)])

    b_out = jnp.swapaxes(basis_out, 1, 2)
    rows32 = jax.ShapeDtypeStruct((32, 128), F32)
    vmem = pl.BlockSpec(memory_space=pltpu.VMEM)
    smem = pl.BlockSpec(memory_space=pltpu.SMEM)
    raw = pl.BlockSpec(memory_space=pl.ANY)
    keep, give, cot_v = pl.pallas_call(
        project_kernel,
        out_shape=[rows32, rows32, pltpu.VMEM(cube, BF16)],
        in_specs=[raw] * 5,
        out_specs=[vmem] * 3,
        scratch_shapes=[
            pltpu.VMEM(cube, BF16),
            pltpu.VMEM((blocks, 16, 128), BF16),
            pltpu.VMEM((blocks, 16, 128), BF16),
            pltpu.VMEM((256, 256), F32),
            pltpu.SemaphoreType.DMA((PARTS + 1, 4)),
        ],
        compiler_params=params(14, None),
        name="project",
    )(
        hbm(features.reshape(cube)),
        hbm(cotangent.reshape(cube)),
        hbm(basis_in),
        hbm(b_out),
        hbm(channel_mix),
    )
    got = lax.ppermute(give, "chan", [(0, 1), (1, 0)])
    msgs = pl.pallas_call(
        deal_kernel,
        out_shape=[jax.ShapeDtypeStruct((56, 128), F32)] * 4,
        in_specs=[smem, vmem, vmem, vmem],
        compiler_params=params(6, None),
        name="deal",
    )(far_index, far_kernel.reshape(128, 16), keep, got)
    seen = [msgs[0]]
    for o in range(1, 4):
        seen.append(lax.ppermute(msgs[o], "curve", [(i, i ^ o) for i in range(groups)]))

    prev, acc = pl.pallas_call(
        backward_kernel,
        out_shape=[
            jax.ShapeDtypeStruct(cube, BF16),
            pltpu.VMEM((2 * blocks + 1, 128, 128), F32),
        ],
        in_specs=[smem, smem, raw, vmem],
        out_specs=[vmem, vmem],
        scratch_shapes=[pltpu.VMEM(near_kernel.shape, BF16), pltpu.SemaphoreType.DMA((CHUNKS,))],
        compiler_params=params(16, None),
        cost_estimate=pl.CostEstimate(flops=8 << 30, bytes_accessed=12 << 20, transcendentals=0),
        name="backward",
    )(index, near_count, hbm(near_kernel), cot_v)
    arrived = lax.ppermute(prev, "curve", [(i + 1, i) for i in range(groups - 1)])

    out_msg, couple, own = pl.pallas_call(
        spread_kernel,
        out_shape=[
            jax.ShapeDtypeStruct((places, 32, 128), BF16),
            pltpu.HBM((2, places * 16, 128), F32),
            pltpu.HBM(cube, F32),
        ],
        in_specs=[vmem] * 5,
        out_specs=[vmem, vmem, raw],
        scratch_shapes=[pltpu.VMEM((4, 24, 128), F32), pltpu.SemaphoreType.DMA],
        compiler_params=params(6, None),
        name="spread",
    )(*seen, acc)
    rings = [[t * QUAD + s for t in range(places)] for s in range(QUAD)]
    in_msg = lax.all_to_all(out_msg, "curve", 0, 0, tiled=True, axis_index_groups=rings)

    near = pl.pallas_call(
        forward_kernel,
        out_shape=pltpu.HBM(cube, F32),
        in_specs=[smem, smem, raw, raw, raw],
        out_specs=raw,
        scratch_shapes=[
            pltpu.VMEM((2 * blocks + 1, 128, 128), BF16),
            pltpu.VMEM(near_kernel.shape, BF16),
            pltpu.VMEM(cube, F32),
            pltpu.SemaphoreType.DMA((CHUNKS,)),
            pltpu.SemaphoreType.DMA((2,)),
            pltpu.SemaphoreType.DMA((CHUNKS,)),
        ],
        compiler_params=params(16, None),
        cost_estimate=pl.CostEstimate(flops=8 << 30, bytes_accessed=12 << 20, transcendentals=0),
        name="forward",
    )(index, near_count, hbm(near_kernel), hbm(halo.reshape(cube)), hbm(features.reshape(cube)))

    back = pl.pallas_call(
        collect_kernel,
        out_shape=[jax.ShapeDtypeStruct((32, 128), BF16)] * 4,
        scratch_shapes=[pltpu.VMEM((256, 128), F32), pltpu.VMEM((16, 128), F32)],
        compiler_params=params(6, None),
        name="collect",
    )(in_msg, couple)
    near_back, own_back = pl.pallas_call(
        fetch_kernel,
        out_shape=[pltpu.VMEM(cube, F32)] * 2,
        in_specs=[raw, raw],
        out_specs=[vmem, vmem],
        scratch_shapes=[pltpu.SemaphoreType.DMA((2,))],
        compiler_params=params(6, None),
        cost_estimate=pl.CostEstimate(flops=1 << 20, bytes_accessed=8 << 20, transcendentals=0),
        name="fetch",
    )(hbm(near), hbm(own))
    home = [back[0]]
    for o in range(1, 4):
        home.append(lax.ppermute(back[o], "curve", [(i, i ^ o) for i in range(groups)]))

    layer, grad = pl.pallas_call(
        finish_kernel,
        out_shape=[pltpu.HBM(cube, BF16)] * 2,
        in_specs=[vmem] * 9,
        out_specs=[raw, raw],
        scratch_shapes=[
            pltpu.VMEM(cube, BF16),
            pltpu.VMEM(cube, BF16),
            pltpu.SemaphoreType.DMA((PARTS, 2)),
        ],
        compiler_params=params(14, None),
        name="finish",
    )(near_back, own_back, arrived, basis_in, b_out, *home)
    return (layer.reshape(features.shape), grad.reshape(features.shape))


def solution(mesh):
    return jax.shard_map(
        layer_step,
        mesh=mesh,
        in_specs=(
            P("curve", "chan"),
            P("curve", "chan"),
            P("curve", None, None, None),
            P("curve", None),
            P("curve"),
            P("curve", None, None),
            P("curve", None, None),
            P("curve", None, None, None),
            P("curve", None),
            P(),
        ),
        out_specs=(P("curve", "chan"), P("curve", "chan")),
        check_vma=False,
    )
```

```python
import jax
import jax.numpy as jnp
from jax import lax
from jax.experimental import pallas as pl
from jax.experimental.pallas import tpu as pltpu
from jax.sharding import PartitionSpec as P


F32 = jnp.float32
BF16 = jnp.bfloat16
MIB = 1 << 20
QUAD = 4
PARTS = 4
CHUNKS = 8
UNROLL = 4


def params(mib, semantics=("arbitrary",)):
    return pltpu.CompilerParams(dimension_semantics=semantics, vmem_limit_bytes=mib * MIB)


def dot(a, b, dims=(((1,), (0,)), ((), ()))):
    return lax.dot_general(a, b, dims, preferred_element_type=F32)


def split(value):
    high = value.astype(BF16)
    return high, (value - high.astype(F32)).astype(BF16)


def hbm(value):
    return pltpu.with_memory_space_constraint(value, pltpu.HBM)


def lanes(shape):
    return lax.broadcasted_iota(jnp.int32, shape, 1)


def moved(value, block, keep):
    rolled = pltpu.roll(value, lax.rem(block * 32 + 256, 128), 1)
    return jnp.where(lanes(value.shape) // 32 == keep, rolled, 0.0)


def project_kernel(feat, cot, b_in, b_out, mix, keep, give, cot_v, feat_lo, feat_hi, b_in_v, b_out_v, mix_v, sems):
    count = feat.shape[0]
    part = count // PARTS
    loads = []
    for n in range(PARTS):
        rows = pl.ds(n * part, part)
        feat_v = (feat_lo, feat_hi)[n // 2].at[pl.ds(n % 2 * part, part)]
        loads.append(
            [
                pltpu.make_async_copy(src.at[rows], dst, sems.at[n, j])
                for j, (src, dst) in enumerate(
                    (
                        (feat, feat_v),
                        (b_in, b_in_v.at[rows]),
                        (cot, cot_v.at[rows]),
                        (b_out, b_out_v.at[rows]),
                    )
                )
            ]
        )
    last = pltpu.make_async_copy(mix, mix_v, sems.at[PARTS, 0])
    for copy in [c for group in loads for c in group] + [last]:
        copy.start()

    acc_f = jnp.zeros((16, 128), F32)
    acc_b = jnp.zeros((16, 128), F32)
    for n in range(PARTS):
        for copy in loads[n]:
            copy.wait()
        picks = range(n * part, (n + 1) * part)
        acc_f += dot(
            jnp.concatenate([b_in_v[i] for i in picks], axis=1),
            (feat_lo, feat_hi)[n // 2][n % 2 * part : (n % 2 + 1) * part].reshape(part * 128, 128),
        )
        acc_b += dot(
            jnp.concatenate([b_out_v[i] for i in picks], axis=1),
            cot_v[n * part : (n + 1) * part].reshape(part * 128, 128),
        )
    last.wait()
    half = lax.axis_index("chan")
    start = pl.multiple_of(half * 128, 128)
    exact = lax.Precision.HIGHEST
    coarse = acc_f.astype(BF16).astype(F32)
    for oh, out in enumerate((keep, give)):
        there = pl.multiple_of((half ^ oh) * 128, 128)
        out[0:16, :] = jnp.dot(
            coarse,
            mix_v[pl.ds(start, 128), pl.ds(there, 128)],
            precision=exact,
            preferred_element_type=F32,
        )
        out[16:32, :] = lax.dot_general(
            acc_b,
            mix_v[pl.ds(there, 128), pl.ds(start, 128)],
            (((1,), (1,)), ((), ())),
            precision=exact,
            preferred_element_type=F32,
        )


def deal_kernel(far_index, far, keep, got, *outs):
    me = lax.rem(lax.axis_index("curve"), QUAD)
    both = keep[...] + got[...]
    wide = jnp.concatenate([far[...], jnp.zeros((128, 112), F32)], axis=1)
    pack = wide.T[0:16]
    lane = lanes((8, 128)) // 16
    row = jnp.zeros((8, 128), jnp.int32)
    for a in range(8):
        row = jnp.where(lane == a, far_index[0, a], row)
    for os in range(4):
        outs[os][0:32, :] = moved(both, me - (me ^ os), me)
        outs[os][32:48, :] = pack
        outs[os][48:56, :] = row.astype(F32)


def tile_loads(near, near_v, sems):
    part = near.shape[0] // CHUNKS
    copies = []
    for n in range(CHUNKS):
        rows = pl.ds(n * part, part)
        copies.append(pltpu.make_async_copy(near.at[rows], near_v.at[rows], sems.at[n]))
        copies[-1].start()
    return copies


def backward_kernel(index, count, near, cot, prev, acc, near_v, sems):
    base = (lax.axis_index("curve") - 1) * 32
    copies = tile_loads(near, near_v, sems)
    acc[...] = jnp.zeros_like(acc)
    part = near.shape[0] // CHUNKS
    for n, copy in enumerate(copies):
        copy.wait()

        def some(step, carry):
            for i in range(UNROLL):
                b = n * part + step * UNROLL + i
                cot_t = cot[b].T
                live = count[b]
                for k in range(0, 8, 2):
                    pair = jnp.concatenate([near_v[b, k], near_v[b, k + 1]], axis=1)
                    term = dot(cot_t, pair)
                    for j in range(2):
                        row = jnp.where(k + j < live, index[k + j, b] - base, 64)
                        acc[row] += term[:, j * 128 : (j + 1) * 128]
            return carry

        lax.fori_loop(0, part // UNROLL, some, 0)
    prev[...] = acc[0:32].astype(BF16)


def forward_kernel(index, count, near, halo_lo, halo_hi, feat, out, rows, near_v, out_v, sems, row_sems, out_sems):
    base = (lax.axis_index("curve") - 1) * 32
    heads = [
        pltpu.make_async_copy(feat, rows.at[pl.ds(32, 32)], row_sems.at[0]),
        pltpu.make_async_copy(halo_lo, rows.at[pl.ds(0, 16)], row_sems.at[1]),
        pltpu.make_async_copy(halo_hi, rows.at[pl.ds(16, 16)], row_sems.at[2]),
    ]
    for copy in heads:
        copy.start()
    copies = tile_loads(near, near_v, sems)
    rows[64] = jnp.zeros((128, 128), BF16)
    for copy in heads:
        copy.wait()
    part = near.shape[0] // CHUNKS
    stores = []
    for n, copy in enumerate(copies):
        copy.wait()

        def some(step, carry):
            for i in range(UNROLL):
                b = n * part + step * UNROLL + i
                live = count[b]
                picked = [rows[jnp.where(k < live, index[k, b] - base, 64)] for k in range(8)]
                tiles = jnp.concatenate([near_v[b, k] for k in range(8)], axis=1)
                out_v[b] = dot(tiles, jnp.concatenate(picked, axis=0))
            return carry

        lax.fori_loop(0, part // UNROLL, some, 0)
        span = pl.ds(n * part, part)
        stores.append(pltpu.make_async_copy(out_v.at[span], out.at[span], out_sems.at[n]))
        stores[-1].start()
    for copy in stores:
        copy.wait()


def fill_couple(msgs, couple, total):
    me = lax.rem(lax.axis_index("curve"), QUAD)
    lane = lanes((24, 128))
    for os in range(4):
        total[me ^ os] = msgs[os][32:56, :]
    packed = []
    for a in range(8):
        group = jnp.zeros((24, 128), F32)
        for g in range(4):
            rolled = pltpu.roll(total[g], (16 * (g - a)) % 128, 1)
            group = jnp.where(lane // 16 == g, rolled, group)
        packed.append(group + pltpu.roll(group, 64, 1))
    lane8 = lanes((8, 128))
    for p in range(2):
        quarter = ((lane8 // 16) % 4 + lane8 // 64 + 2 * p) % 4
        wants = [packed[a][16:24].astype(jnp.int32) - quarter for a in range(8)]
        for t in range(32):
            tile = jnp.zeros((16, 128), F32)
            for a in range(8):
                hit = wants[a] == 4 * t
                hit = jnp.concatenate([hit, hit], axis=0)
                tile = tile + jnp.where(hit, packed[a][0:16], 0.0)
            couple[p, t * 16 : (t + 1) * 16, :] = tile


def couple_kernel(*refs):
    fill_couple(refs[:4], refs[4], refs[5])


def spread_kernel(*refs):
    msgs, acc, (out, own), (total, couple, sem) = refs[:4], refs[4], refs[5:7], refs[7:]
    saved = pltpu.make_async_copy(acc.at[pl.ds(32, 32)], own, sem)
    saved.start()
    fill_couple(msgs, couple, total)
    value = msgs[0][0:32, :]
    for ref in msgs[1:]:
        value = value + ref[0:32, :]
    fwd = value[0:16].astype(BF16)
    bwd = value[16:32]
    lane16 = lanes((16, 128))
    block = jnp.concatenate(
        [jnp.where(lane16 // 32 == g, bwd, 0.0) for g in range(4)], axis=0
    )
    contrib = jnp.zeros((512, 128), F32)
    for p in range(2):
        rhs = jnp.concatenate(
            [block if d == 0 else pltpu.roll(block, 32 * d, 1) for d in (2 * p, 2 * p + 1)],
            axis=0,
        )
        r_hi, r_lo = split(rhs)
        k_hi, k_lo = split(couple[p])
        contrib = contrib + (dot(k_hi, r_lo) + dot(k_lo, r_hi)) + dot(k_hi, r_hi)
    contrib = contrib.astype(BF16)
    for t in range(32):
        out[t, 0:16, :] = fwd
        out[t, 16:32, :] = contrib[t * 16 : (t + 1) * 16]
    saved.wait()


def collect_kernel(arrived, couple, *refs):
    outs, (picked, summed) = refs[:4], refs[4:]
    me = lax.rem(lax.axis_index("curve"), QUAD)
    total = arrived[0, 16:32, :].astype(F32)
    for t in range(1, 32):
        total = total + arrived[t, 16:32, :].astype(F32)
    source = jnp.concatenate([arrived[t, 0:16, :] for t in range(32)], axis=0)
    over_rows = (((0,), (0,)), ((), ()))
    for p in range(2):
        k_hi, k_lo = split(couple[p])
        picked[p * 128 : (p + 1) * 128, :] = dot(k_hi, source, over_rows) + dot(
            k_lo, source, over_rows
        )
    for os in range(4):
        owner = me ^ os
        far = jnp.zeros((16, 128), F32)
        for d in range(4):
            rows = picked[pl.ds(pl.multiple_of(d * 64 + owner * 16, 16), 16), :]
            far = far + moved(rows, me - owner - d, me)
        outs[os][0:16, :] = far.astype(BF16)
        outs[os][16:32, :] = moved(total, me - owner, me).astype(BF16)


def fetch_kernel(near, own, near_v, own_v, sems):
    copies = [
        pltpu.make_async_copy(near, near_v, sems.at[0]),
        pltpu.make_async_copy(own, own_v, sems.at[1]),
    ]
    for copy in copies:
        copy.start()
    for copy in copies:
        copy.wait()


def finish_kernel(
    near, own, arrived, b_in, b_out, m0, m1, m2, m3, layer, grad, layer_v, grad_v, sems
):
    value = ((m0[...] + m1[...]) + (m2[...] + m3[...])).astype(BF16)
    far = value[0:16]
    coarse_t = value[16:32].astype(F32).T.astype(BF16)
    copies = []
    part = near.shape[0] // PARTS
    for n in range(PARTS):
        for i in range(n * part, (n + 1) * part):
            term = dot(b_out[i], far, (((0,), (0,)), ((), ())))
            layer_v[i] = (near[i] + term).astype(BF16)
            total = own[i] + arrived[i].astype(F32) + dot(coarse_t, b_in[i])
            grad_v[i] = total.astype(BF16).T
        for j, (src, dst) in enumerate(((layer_v, layer), (grad_v, grad))):
            rows = pl.ds(n * part, part)
            copies.append(pltpu.make_async_copy(src.at[rows], dst.at[rows], sems.at[n, j]))
            copies[-1].start()
    for copy in copies:
        copy.wait()


def layer_step(
    features,
    cotangent,
    near_kernel,
    near_index,
    near_count,
    basis_in,
    basis_out,
    far_kernel,
    far_index,
    channel_mix,
):
    groups = lax.axis_size("curve")
    blocks = near_kernel.shape[0]
    places = groups // QUAD
    index = near_index.T
    cube = (blocks, 128, 128)

    b_out = jnp.swapaxes(basis_out, 1, 2)
    rows32 = jax.ShapeDtypeStruct((32, 128), F32)
    vmem = pl.BlockSpec(memory_space=pltpu.VMEM)
    smem = pl.BlockSpec(memory_space=pltpu.SMEM)
    raw = pl.BlockSpec(memory_space=pl.ANY)
    half_cube = (blocks // 2, 128, 128)
    keep, give, cot_v, feat_lo, feat_hi = pl.pallas_call(
        project_kernel,
        out_shape=[rows32, rows32, pltpu.VMEM(cube, BF16)] + [pltpu.VMEM(half_cube, BF16)] * 2,
        in_specs=[raw] * 5,
        out_specs=[vmem] * 5,
        scratch_shapes=[
            pltpu.VMEM((blocks, 16, 128), BF16),
            pltpu.VMEM((blocks, 16, 128), BF16),
            pltpu.VMEM((256, 256), F32),
            pltpu.SemaphoreType.DMA((PARTS + 1, 4)),
        ],
        compiler_params=params(14, None),
        name="project",
    )(
        hbm(features.reshape(cube)),
        hbm(cotangent.reshape(cube)),
        hbm(basis_in),
        hbm(b_out),
        hbm(channel_mix),
    )
    got = lax.ppermute(give, "chan", [(0, 1), (1, 0)])
    onward = [(i, i + 1) for i in range(groups - 1)]
    halo_lo = lax.ppermute(feat_lo, "curve", onward)
    halo_hi = lax.ppermute(feat_hi, "curve", onward)
    msgs = pl.pallas_call(
        deal_kernel,
        out_shape=[jax.ShapeDtypeStruct((56, 128), F32)] * 4,
        in_specs=[smem, vmem, vmem, vmem],
        compiler_params=params(6, None),
        name="deal",
    )(far_index, far_kernel.reshape(128, 16), keep, got)
    seen = [msgs[0]]
    for o in range(1, 4):
        seen.append(lax.ppermute(msgs[o], "curve", [(i, i ^ o) for i in range(groups)]))

    prev, acc = pl.pallas_call(
        backward_kernel,
        out_shape=[
            jax.ShapeDtypeStruct(cube, BF16),
            pltpu.VMEM((2 * blocks + 1, 128, 128), F32),
        ],
        in_specs=[smem, smem, raw, vmem],
        out_specs=[vmem, vmem],
        scratch_shapes=[pltpu.VMEM(near_kernel.shape, BF16), pltpu.SemaphoreType.DMA((CHUNKS,))],
        compiler_params=params(16, None),
        cost_estimate=pl.CostEstimate(flops=8 << 30, bytes_accessed=12 << 20, transcendentals=0),
        name="backward",
    )(index, near_count, hbm(near_kernel), cot_v)
    arrived = lax.ppermute(prev, "curve", [(i + 1, i) for i in range(groups - 1)])

    out_msg, own = pl.pallas_call(
        spread_kernel,
        out_shape=[
            jax.ShapeDtypeStruct((places, 32, 128), BF16),
            pltpu.HBM(cube, F32),
        ],
        in_specs=[vmem] * 5,
        out_specs=[vmem, raw],
        scratch_shapes=[
            pltpu.VMEM((4, 24, 128), F32),
            pltpu.VMEM((2, places * 16, 128), F32),
            pltpu.SemaphoreType.DMA,
        ],
        compiler_params=params(6, None),
        name="spread",
    )(*seen, acc)
    rings = [[t * QUAD + s for t in range(places)] for s in range(QUAD)]
    in_msg = lax.all_to_all(out_msg, "curve", 0, 0, tiled=True, axis_index_groups=rings)

    couple = pl.pallas_call(
        couple_kernel,
        out_shape=pltpu.HBM((2, places * 16, 128), F32),
        scratch_shapes=[pltpu.VMEM((4, 24, 128), F32)],
        compiler_params=params(6, None),
        cost_estimate=pl.CostEstimate(flops=1 << 20, bytes_accessed=1 << 20, transcendentals=0),
        name="couple",
    )(*seen)

    near = pl.pallas_call(
        forward_kernel,
        out_shape=pltpu.HBM(cube, F32),
        in_specs=[smem, smem, raw, raw, raw, raw],
        out_specs=raw,
        scratch_shapes=[
            pltpu.VMEM((2 * blocks + 1, 128, 128), BF16),
            pltpu.VMEM(near_kernel.shape, BF16),
            pltpu.VMEM(cube, F32),
            pltpu.SemaphoreType.DMA((CHUNKS,)),
            pltpu.SemaphoreType.DMA((3,)),
            pltpu.SemaphoreType.DMA((CHUNKS,)),
        ],
        compiler_params=params(16, None),
        cost_estimate=pl.CostEstimate(flops=8 << 30, bytes_accessed=12 << 20, transcendentals=0),
        name="forward",
    )(index, near_count, hbm(near_kernel), hbm(halo_lo), hbm(halo_hi), hbm(features.reshape(cube)))

    back = pl.pallas_call(
        collect_kernel,
        out_shape=[jax.ShapeDtypeStruct((32, 128), BF16)] * 4,
        scratch_shapes=[pltpu.VMEM((256, 128), F32), pltpu.VMEM((16, 128), F32)],
        compiler_params=params(6, None),
        name="collect",
    )(in_msg, couple)
    near_back, own_back = pl.pallas_call(
        fetch_kernel,
        out_shape=[pltpu.VMEM(cube, F32)] * 2,
        in_specs=[raw, raw],
        out_specs=[vmem, vmem],
        scratch_shapes=[pltpu.SemaphoreType.DMA((2,))],
        compiler_params=params(6, None),
        cost_estimate=pl.CostEstimate(flops=1 << 20, bytes_accessed=8 << 20, transcendentals=0),
        name="fetch",
    )(hbm(near), hbm(own))
    home = [back[0]]
    for o in range(1, 4):
        home.append(lax.ppermute(back[o], "curve", [(i, i ^ o) for i in range(groups)]))

    layer, grad = pl.pallas_call(
        finish_kernel,
        out_shape=[pltpu.HBM(cube, BF16)] * 2,
        in_specs=[vmem] * 9,
        out_specs=[raw, raw],
        scratch_shapes=[
            pltpu.VMEM(cube, BF16),
            pltpu.VMEM(cube, BF16),
            pltpu.SemaphoreType.DMA((PARTS, 2)),
        ],
        compiler_params=params(14, None),
        name="finish",
    )(near_back, own_back, arrived, basis_in, b_out, *home)
    return (layer.reshape(features.shape), grad.reshape(features.shape))


def solution(mesh):
    return jax.shard_map(
        layer_step,
        mesh=mesh,
        in_specs=(
            P("curve", "chan"),
            P("curve", "chan"),
            P("curve", None, None, None),
            P("curve", None),
            P("curve"),
            P("curve", None, None),
            P("curve", None, None),
            P("curve", None, None, None),
            P("curve", None),
            P(),
        ),
        out_specs=(P("curve", "chan"), P("curve", "chan")),
        check_vma=False,
    )
```

```python
import jax
import jax.numpy as jnp
from jax import lax
from jax.experimental import pallas as pl
from jax.experimental.pallas import tpu as pltpu
from jax.sharding import PartitionSpec as P


F32 = jnp.float32
BF16 = jnp.bfloat16
MIB = 1 << 20
QUAD = 4
PARTS = 4
CHUNKS = 8
AHEAD = 3


def params(mib, semantics=("arbitrary",)):
    return pltpu.CompilerParams(dimension_semantics=semantics, vmem_limit_bytes=mib * MIB)


def dot(a, b, dims=(((1,), (0,)), ((), ()))):
    return lax.dot_general(a, b, dims, preferred_element_type=F32)


def split(value):
    high = value.astype(BF16)
    return high, (value - high.astype(F32)).astype(BF16)


def hbm(value):
    return pltpu.with_memory_space_constraint(value, pltpu.HBM)


def lanes(shape):
    return lax.broadcasted_iota(jnp.int32, shape, 1)


def moved(value, block, keep):
    rolled = pltpu.roll(value, lax.rem(block * 32 + 256, 128), 1)
    return jnp.where(lanes(value.shape) // 32 == keep, rolled, 0.0)


def project_kernel(feat, cot, b_in, b_out, mix, keep, give, cot_v, feat_v, b_in_v, b_out_v, mix_v, sems):
    count = feat.shape[0]
    part = count // PARTS
    loads = []
    for n in range(PARTS):
        rows = pl.ds(n * part, part)
        loads.append(
            [
                pltpu.make_async_copy(src.at[rows], dst, sems.at[n, j])
                for j, (src, dst) in enumerate(
                    (
                        (feat, feat_v.at[rows]),
                        (b_in, b_in_v.at[rows]),
                        (cot, cot_v.at[rows]),
                        (b_out, b_out_v.at[rows]),
                    )
                )
            ]
        )
    last = pltpu.make_async_copy(mix, mix_v, sems.at[PARTS, 0])
    for copy in [c for group in loads for c in group] + [last]:
        copy.start()

    acc_f = jnp.zeros((16, 128), F32)
    acc_b = jnp.zeros((16, 128), F32)
    for n in range(PARTS):
        for copy in loads[n]:
            copy.wait()
        picks = range(n * part, (n + 1) * part)
        acc_f += dot(
            jnp.concatenate([b_in_v[i] for i in picks], axis=1),
            feat_v[n * part : (n + 1) * part].reshape(part * 128, 128),
        )
        acc_b += dot(
            jnp.concatenate([b_out_v[i] for i in picks], axis=1),
            cot_v[n * part : (n + 1) * part].reshape(part * 128, 128),
        )
    last.wait()
    half = lax.axis_index("chan")
    start = pl.multiple_of(half * 128, 128)
    exact = lax.Precision.HIGHEST
    coarse = acc_f.astype(BF16).astype(F32)
    for oh, out in enumerate((keep, give)):
        there = pl.multiple_of((half ^ oh) * 128, 128)
        out[0:16, :] = jnp.dot(
            coarse,
            mix_v[pl.ds(start, 128), pl.ds(there, 128)],
            precision=exact,
            preferred_element_type=F32,
        )
        out[16:32, :] = lax.dot_general(
            acc_b,
            mix_v[pl.ds(there, 128), pl.ds(start, 128)],
            (((1,), (1,)), ((), ())),
            precision=exact,
            preferred_element_type=F32,
        )


def deal_kernel(far_index, far, keep, got, *outs):
    me = lax.rem(lax.axis_index("curve"), QUAD)
    both = keep[...] + got[...]
    wide = jnp.concatenate([far[...], jnp.zeros((128, 112), F32)], axis=1)
    pack = wide.T[0:16]
    lane = lanes((8, 128)) // 16
    row = jnp.zeros((8, 128), jnp.int32)
    for a in range(8):
        row = jnp.where(lane == a, far_index[0, a], row)
    for os in range(4):
        outs[os][0:32, :] = moved(both, me - (me ^ os), me)
        outs[os][32:48, :] = pack
        outs[os][48:56, :] = row.astype(F32)


def tile_copies(near, near_v, sems):
    part = near.shape[0] // CHUNKS
    spans = [pl.ds(n * part, part) for n in range(CHUNKS)]
    return [
        pltpu.make_async_copy(near.at[span], near_v.at[span], sems.at[n])
        for n, span in enumerate(spans)
    ]


def backward_kernel(index, count, near, cot, prev, own, acc, near_v, sems, out_sems):
    base = (lax.axis_index("curve") - 1) * 32
    copies = tile_copies(near, near_v, sems)[::-1]
    for copy in copies[:AHEAD]:
        copy.start()
    acc[...] = jnp.zeros_like(acc)
    part = near.shape[0] // CHUNKS
    stores = []
    for turn, copy in enumerate(copies):
        copy.wait()
        if turn + AHEAD < CHUNKS:
            copies[turn + AHEAD].start()
        n = CHUNKS - 1 - turn
        for b in range(n * part, (n + 1) * part):
            cot_t = cot[b].T
            live = count[b]
            for k in range(0, 8, 2):
                pair = jnp.concatenate([near_v[b, k], near_v[b, k + 1]], axis=1)
                term = dot(cot_t, pair)
                for j in range(2):
                    row = jnp.where(k + j < live, index[k + j, b] - base, 64)
                    acc[row] += term[:, j * 128 : (j + 1) * 128]
        done = acc.at[pl.ds(32 + n * part, part)]
        stores.append(pltpu.make_async_copy(done, own.at[pl.ds(n * part, part)], out_sems.at[n]))
        stores[-1].start()
    prev[...] = acc[0:32].astype(BF16)
    for copy in stores:
        copy.wait()


def forward_kernel(index, count, near, halo, feat, out, rows, near_v, out_v, sems, row_sems, out_sems):
    base = (lax.axis_index("curve") - 1) * 32
    heads = [
        pltpu.make_async_copy(feat, rows.at[pl.ds(32, 32)], row_sems.at[0]),
        pltpu.make_async_copy(halo, rows.at[pl.ds(0, 32)], row_sems.at[1]),
    ]
    copies = tile_copies(near, near_v, sems)
    for copy in heads + copies[:1]:
        copy.start()
    rows[64] = jnp.zeros((128, 128), BF16)
    for copy in heads:
        copy.wait()
    for copy in copies[1:AHEAD]:
        copy.start()
    part = near.shape[0] // CHUNKS
    stores = []
    for n, copy in enumerate(copies):
        copy.wait()
        if n + AHEAD < CHUNKS:
            copies[n + AHEAD].start()
        for b in range(n * part, (n + 1) * part):
            live = count[b]
            picked = [rows[jnp.where(k < live, index[k, b] - base, 64)] for k in range(8)]
            tiles = jnp.concatenate([near_v[b, k] for k in range(8)], axis=1)
            out_v[b] = dot(tiles, jnp.concatenate(picked, axis=0))
        span = pl.ds(n * part, part)
        stores.append(pltpu.make_async_copy(out_v.at[span], out.at[span], out_sems.at[n]))
        stores[-1].start()
    for copy in stores:
        copy.wait()


def fill_couple(msgs, couple, total):
    me = lax.rem(lax.axis_index("curve"), QUAD)
    lane = lanes((24, 128))
    for os in range(4):
        total[me ^ os] = msgs[os][32:56, :]
    packed = []
    for a in range(8):
        group = jnp.zeros((24, 128), F32)
        for g in range(4):
            rolled = pltpu.roll(total[g], (16 * (g - a)) % 128, 1)
            group = jnp.where(lane // 16 == g, rolled, group)
        packed.append(group + pltpu.roll(group, 64, 1))
    lane8 = lanes((8, 128))
    for p in range(2):
        quarter = ((lane8 // 16) % 4 + lane8 // 64 + 2 * p) % 4
        wants = [packed[a][16:24].astype(jnp.int32) - quarter for a in range(8)]
        for t in range(32):
            tile = jnp.zeros((16, 128), F32)
            for a in range(8):
                hit = wants[a] == 4 * t
                hit = jnp.concatenate([hit, hit], axis=0)
                tile = tile + jnp.where(hit, packed[a][0:16], 0.0)
            couple[p, t * 16 : (t + 1) * 16, :] = tile


def spread_kernel(*refs):
    msgs, out, (total, couple) = refs[:4], refs[4], refs[5:]
    fill_couple(msgs, couple, total)
    value = msgs[0][0:32, :]
    for ref in msgs[1:]:
        value = value + ref[0:32, :]
    fwd = value[0:16].astype(BF16)
    bwd = value[16:32]
    lane16 = lanes((16, 128))
    block = jnp.concatenate(
        [jnp.where(lane16 // 32 == g, bwd, 0.0) for g in range(4)], axis=0
    )
    contrib = jnp.zeros((512, 128), F32)
    for p in range(2):
        rhs = jnp.concatenate(
            [block if d == 0 else pltpu.roll(block, 32 * d, 1) for d in (2 * p, 2 * p + 1)],
            axis=0,
        )
        r_hi, r_lo = split(rhs)
        k_hi, k_lo = split(couple[p])
        contrib = contrib + (dot(k_hi, r_lo) + dot(k_lo, r_hi)) + dot(k_hi, r_hi)
    contrib = contrib.astype(BF16)
    for t in range(32):
        out[t, 0:16, :] = fwd
        out[t, 16:32, :] = contrib[t * 16 : (t + 1) * 16]


def collect_kernel(arrived, *refs):
    msgs, outs, (picked, groups, couple) = refs[:4], refs[4:8], refs[8:]
    fill_couple(msgs, couple, groups)
    me = lax.rem(lax.axis_index("curve"), QUAD)
    total = arrived[0, 16:32, :].astype(F32)
    for t in range(1, 32):
        total = total + arrived[t, 16:32, :].astype(F32)
    source = jnp.concatenate([arrived[t, 0:16, :] for t in range(32)], axis=0)
    over_rows = (((0,), (0,)), ((), ()))
    for p in range(2):
        k_hi, k_lo = split(couple[p])
        picked[p * 128 : (p + 1) * 128, :] = dot(k_hi, source, over_rows) + dot(
            k_lo, source, over_rows
        )
    for os in range(4):
        owner = me ^ os
        far = jnp.zeros((16, 128), F32)
        for d in range(4):
            rows = picked[pl.ds(pl.multiple_of(d * 64 + owner * 16, 16), 16), :]
            far = far + moved(rows, me - owner - d, me)
        outs[os][0:16, :] = far.astype(BF16)
        outs[os][16:32, :] = moved(total, me - owner, me).astype(BF16)


def fetch_kernel(near, own, near_v, own_v, sems):
    copies = [
        pltpu.make_async_copy(near, near_v, sems.at[0]),
        pltpu.make_async_copy(own, own_v, sems.at[1]),
    ]
    for copy in copies:
        copy.start()
    for copy in copies:
        copy.wait()


def finish_kernel(
    near, own, arrived, b_in, b_out, m0, m1, m2, m3, layer, grad, layer_v, grad_v, sems
):
    value = ((m0[...] + m1[...]) + (m2[...] + m3[...])).astype(BF16)
    far = value[0:16]
    coarse_t = value[16:32].astype(F32).T.astype(BF16)
    copies = []
    part = near.shape[0] // PARTS
    for n in range(PARTS):
        for i in range(n * part, (n + 1) * part):
            term = dot(b_out[i], far, (((0,), (0,)), ((), ())))
            layer_v[i] = (near[i] + term).astype(BF16)
            total = own[i] + arrived[i].astype(F32) + dot(coarse_t, b_in[i])
            grad_v[i] = total.astype(BF16).T
        for j, (src, dst) in enumerate(((layer_v, layer), (grad_v, grad))):
            rows = pl.ds(n * part, part)
            copies.append(pltpu.make_async_copy(src.at[rows], dst.at[rows], sems.at[n, j]))
            copies[-1].start()
    for copy in copies:
        copy.wait()


def layer_step(
    features,
    cotangent,
    near_kernel,
    near_index,
    near_count,
    basis_in,
    basis_out,
    far_kernel,
    far_index,
    channel_mix,
):
    groups = lax.axis_size("curve")
    blocks = near_kernel.shape[0]
    places = groups // QUAD
    index = near_index.T
    cube = (blocks, 128, 128)

    b_out = jnp.swapaxes(basis_out, 1, 2)
    rows32 = jax.ShapeDtypeStruct((32, 128), F32)
    vmem = pl.BlockSpec(memory_space=pltpu.VMEM)
    smem = pl.BlockSpec(memory_space=pltpu.SMEM)
    raw = pl.BlockSpec(memory_space=pl.ANY)
    keep, give, cot_v = pl.pallas_call(
        project_kernel,
        out_shape=[rows32, rows32, pltpu.VMEM(cube, BF16)],
        in_specs=[raw] * 5,
        out_specs=[vmem] * 3,
        scratch_shapes=[
            pltpu.VMEM(cube, BF16),
            pltpu.VMEM((blocks, 16, 128), BF16),
            pltpu.VMEM((blocks, 16, 128), BF16),
            pltpu.VMEM((256, 256), F32),
            pltpu.SemaphoreType.DMA((PARTS + 1, 4)),
        ],
        compiler_params=params(14, None),
        name="project",
    )(
        hbm(features.reshape(cube)),
        hbm(cotangent.reshape(cube)),
        hbm(basis_in),
        hbm(b_out),
        hbm(channel_mix),
    )
    got = lax.ppermute(give, "chan", [(0, 1), (1, 0)])
    halo = lax.ppermute(features, "curve", [(i, i + 1) for i in range(groups - 1)])
    msgs = pl.pallas_call(
        deal_kernel,
        out_shape=[jax.ShapeDtypeStruct((56, 128), F32)] * 4,
        in_specs=[smem, vmem, vmem, vmem],
        compiler_params=params(6, None),
        name="deal",
    )(far_index, far_kernel.reshape(128, 16), keep, got)
    seen = [msgs[0]]
    for o in range(1, 4):
        seen.append(lax.ppermute(msgs[o], "curve", [(i, i ^ o) for i in range(groups)]))

    prev, own = pl.pallas_call(
        backward_kernel,
        out_shape=[jax.ShapeDtypeStruct(cube, BF16), pltpu.HBM(cube, F32)],
        in_specs=[smem, smem, raw, vmem],
        out_specs=[vmem, raw],
        scratch_shapes=[
            pltpu.VMEM((2 * blocks + 1, 128, 128), F32),
            pltpu.VMEM(near_kernel.shape, BF16),
            pltpu.SemaphoreType.DMA((CHUNKS,)),
            pltpu.SemaphoreType.DMA((CHUNKS,)),
        ],
        compiler_params=params(16, None),
        cost_estimate=pl.CostEstimate(flops=8 << 30, bytes_accessed=12 << 20, transcendentals=0),
        name="backward",
    )(index, near_count, hbm(near_kernel), cot_v)
    arrived = lax.ppermute(prev, "curve", [(i + 1, i) for i in range(groups - 1)])

    out_msg = pl.pallas_call(
        spread_kernel,
        out_shape=jax.ShapeDtypeStruct((places, 32, 128), BF16),
        scratch_shapes=[
            pltpu.VMEM((4, 24, 128), F32),
            pltpu.VMEM((2, places * 16, 128), F32),
        ],
        compiler_params=params(6, None),
        name="spread",
    )(*seen)
    rings = [[t * QUAD + s for t in range(places)] for s in range(QUAD)]
    in_msg = lax.all_to_all(out_msg, "curve", 0, 0, tiled=True, axis_index_groups=rings)

    near = pl.pallas_call(
        forward_kernel,
        out_shape=pltpu.HBM(cube, F32),
        in_specs=[smem, smem, raw, raw, raw],
        out_specs=raw,
        scratch_shapes=[
            pltpu.VMEM((2 * blocks + 1, 128, 128), BF16),
            pltpu.VMEM(near_kernel.shape, BF16),
            pltpu.VMEM(cube, F32),
            pltpu.SemaphoreType.DMA((CHUNKS,)),
            pltpu.SemaphoreType.DMA((2,)),
            pltpu.SemaphoreType.DMA((CHUNKS,)),
        ],
        compiler_params=params(16, None),
        cost_estimate=pl.CostEstimate(flops=8 << 30, bytes_accessed=12 << 20, transcendentals=0),
        name="forward",
    )(index, near_count, hbm(near_kernel), hbm(halo.reshape(cube)), hbm(features.reshape(cube)))

    back = pl.pallas_call(
        collect_kernel,
        out_shape=[jax.ShapeDtypeStruct((32, 128), BF16)] * 4,
        scratch_shapes=[
            pltpu.VMEM((256, 128), F32),
            pltpu.VMEM((4, 24, 128), F32),
            pltpu.VMEM((2, places * 16, 128), F32),
        ],
        compiler_params=params(6, None),
        name="collect",
    )(in_msg, *seen)
    near_back, own_back = pl.pallas_call(
        fetch_kernel,
        out_shape=[pltpu.VMEM(cube, F32)] * 2,
        in_specs=[raw, raw],
        out_specs=[vmem, vmem],
        scratch_shapes=[pltpu.SemaphoreType.DMA((2,))],
        compiler_params=params(6, None),
        cost_estimate=pl.CostEstimate(flops=1 << 20, bytes_accessed=8 << 20, transcendentals=0),
        name="fetch",
    )(hbm(near), hbm(own))
    home = [back[0]]
    for o in range(1, 4):
        home.append(lax.ppermute(back[o], "curve", [(i, i ^ o) for i in range(groups)]))

    layer, grad = pl.pallas_call(
        finish_kernel,
        out_shape=[pltpu.HBM(cube, BF16)] * 2,
        in_specs=[vmem] * 9,
        out_specs=[raw, raw],
        scratch_shapes=[
            pltpu.VMEM(cube, BF16),
            pltpu.VMEM(cube, BF16),
            pltpu.SemaphoreType.DMA((PARTS, 2)),
        ],
        compiler_params=params(14, None),
        name="finish",
    )(near_back, own_back, arrived, basis_in, b_out, *home)
    return (layer.reshape(features.shape), grad.reshape(features.shape))


def solution(mesh):
    return jax.shard_map(
        layer_step,
        mesh=mesh,
        in_specs=(
            P("curve", "chan"),
            P("curve", "chan"),
            P("curve", None, None, None),
            P("curve", None),
            P("curve"),
            P("curve", None, None),
            P("curve", None, None),
            P("curve", None, None, None),
            P("curve", None),
            P(),
        ),
        out_specs=(P("curve", "chan"), P("curve", "chan")),
        check_vma=False,
    )
```

```python
import jax
import jax.numpy as jnp
from jax import lax
from jax.experimental import pallas as pl
from jax.experimental.pallas import tpu as pltpu
from jax.sharding import PartitionSpec as P


F32 = jnp.float32
BF16 = jnp.bfloat16
MIB = 1 << 20
QUAD = 4
PARTS = 4
UNROLL = 4
CHUNKS = 8
AHEAD = 3


def params(mib, semantics=("arbitrary",)):
    return pltpu.CompilerParams(dimension_semantics=semantics, vmem_limit_bytes=mib * MIB)


def dot(a, b, dims=(((1,), (0,)), ((), ()))):
    return lax.dot_general(a, b, dims, preferred_element_type=F32)


def split(value):
    high = value.astype(BF16)
    return high, (value - high.astype(F32)).astype(BF16)


def hbm(value):
    return pltpu.with_memory_space_constraint(value, pltpu.HBM)


def lanes(shape):
    return lax.broadcasted_iota(jnp.int32, shape, 1)


def moved(value, block, keep):
    rolled = pltpu.roll(value, lax.rem(block * 32 + 256, 128), 1)
    return jnp.where(lanes(value.shape) // 32 == keep, rolled, 0.0)


def project_kernel(feat, cot, b_in, b_out, mix, keep, give, cot_v, feat_v, b_in_v, b_out_v, mix_v, sems):
    count = feat.shape[0]
    part = count // PARTS
    loads = []
    for n in range(PARTS):
        rows = pl.ds(n * part, part)
        loads.append(
            [
                pltpu.make_async_copy(src.at[rows], dst, sems.at[n, j])
                for j, (src, dst) in enumerate(
                    (
                        (feat, feat_v.at[rows]),
                        (b_in, b_in_v.at[rows]),
                        (cot, cot_v.at[rows]),
                        (b_out, b_out_v.at[rows]),
                    )
                )
            ]
        )
    last = pltpu.make_async_copy(mix, mix_v, sems.at[PARTS, 0])
    for copy in [c for group in loads for c in group] + [last]:
        copy.start()

    acc_f = jnp.zeros((16, 128), F32)
    acc_b = jnp.zeros((16, 128), F32)
    for n in range(PARTS):
        for copy in loads[n]:
            copy.wait()
        picks = range(n * part, (n + 1) * part)
        acc_f += dot(
            jnp.concatenate([b_in_v[i] for i in picks], axis=1),
            feat_v[n * part : (n + 1) * part].reshape(part * 128, 128),
        )
        acc_b += dot(
            jnp.concatenate([b_out_v[i] for i in picks], axis=1),
            cot_v[n * part : (n + 1) * part].reshape(part * 128, 128),
        )
    last.wait()
    half = lax.axis_index("chan")
    start = pl.multiple_of(half * 128, 128)
    exact = lax.Precision.HIGHEST
    coarse = acc_f.astype(BF16).astype(F32)
    for oh, out in enumerate((keep, give)):
        there = pl.multiple_of((half ^ oh) * 128, 128)
        out[0:16, :] = jnp.dot(
            coarse,
            mix_v[pl.ds(start, 128), pl.ds(there, 128)],
            precision=exact,
            preferred_element_type=F32,
        )
        out[16:32, :] = lax.dot_general(
            acc_b,
            mix_v[pl.ds(there, 128), pl.ds(start, 128)],
            (((1,), (1,)), ((), ())),
            precision=exact,
            preferred_element_type=F32,
        )


def deal_kernel(far_index, far, keep, got, *outs):
    me = lax.rem(lax.axis_index("curve"), QUAD)
    both = keep[...] + got[...]
    wide = jnp.concatenate([far[...], jnp.zeros((128, 112), F32)], axis=1)
    pack = wide.T[0:16]
    lane = lanes((8, 128)) // 16
    row = jnp.zeros((8, 128), jnp.int32)
    for a in range(8):
        row = jnp.where(lane == a, far_index[0, a], row)
    for os in range(4):
        outs[os][0:32, :] = moved(both, me - (me ^ os), me)
        outs[os][32:48, :] = pack
        outs[os][48:56, :] = row.astype(F32)


def tile_copies(near, near_v, sems):
    part = near.shape[0] // CHUNKS
    spans = [pl.ds(n * part, part) for n in range(CHUNKS)]
    return [
        pltpu.make_async_copy(near.at[span], near_v.at[span], sems.at[n])
        for n, span in enumerate(spans)
    ]


def backward_kernel(index, count, near, cot, prev, own, acc, out_sems):
    base = (lax.axis_index("curve") - 1) * 32
    acc[...] = jnp.zeros_like(acc)
    part = near.shape[0] // PARTS
    stores = []
    for n in reversed(range(PARTS)):

        def some(step, carry):
            for i in range(UNROLL):
                b = (n + 1) * part - 1 - (step * UNROLL + i)
                cot_t = cot[b].T
                live = count[b]
                for k in range(0, 8, 2):
                    pair = jnp.concatenate([near[b, k], near[b, k + 1]], axis=1)
                    term = dot(cot_t, pair)
                    for j in range(2):
                        row = jnp.where(k + j < live, index[k + j, b] - base, 64)
                        acc[row] += term[:, j * 128 : (j + 1) * 128]
            return carry

        lax.fori_loop(0, part // UNROLL, some, 0)
        done = acc.at[pl.ds(32 + n * part, part)]
        stores.append(pltpu.make_async_copy(done, own.at[pl.ds(n * part, part)], out_sems.at[n]))
        stores[-1].start()
    prev[...] = acc[0:32].astype(BF16)
    for copy in stores:
        copy.wait()


def forward_kernel(index, count, near, halo, feat, out, rows, near_v, out_v, sems, row_sems, out_sems):
    base = (lax.axis_index("curve") - 1) * 32
    heads = [
        pltpu.make_async_copy(feat, rows.at[pl.ds(32, 32)], row_sems.at[0]),
        pltpu.make_async_copy(halo, rows.at[pl.ds(0, 32)], row_sems.at[1]),
    ]
    copies = tile_copies(near, near_v, sems)
    for copy in heads + copies[:1]:
        copy.start()
    rows[64] = jnp.zeros((128, 128), BF16)
    for copy in heads:
        copy.wait()
    for copy in copies[1:AHEAD]:
        copy.start()
    part = near.shape[0] // CHUNKS
    stores = []
    for n, copy in enumerate(copies):
        copy.wait()
        if n + AHEAD < CHUNKS:
            copies[n + AHEAD].start()
        for b in range(n * part, (n + 1) * part):
            live = count[b]
            picked = [rows[jnp.where(k < live, index[k, b] - base, 64)] for k in range(8)]
            tiles = jnp.concatenate([near_v[b, k] for k in range(8)], axis=1)
            out_v[b] = dot(tiles, jnp.concatenate(picked, axis=0))
        span = pl.ds(n * part, part)
        stores.append(pltpu.make_async_copy(out_v.at[span], out.at[span], out_sems.at[n]))
        stores[-1].start()
    for copy in stores:
        copy.wait()


def fill_couple(msgs, couple, total):
    me = lax.rem(lax.axis_index("curve"), QUAD)
    lane = lanes((24, 128))
    for os in range(4):
        total[me ^ os] = msgs[os][32:56, :]
    packed = []
    for a in range(8):
        group = jnp.zeros((24, 128), F32)
        for g in range(4):
            rolled = pltpu.roll(total[g], (16 * (g - a)) % 128, 1)
            group = jnp.where(lane // 16 == g, rolled, group)
        packed.append(group + pltpu.roll(group, 64, 1))
    lane8 = lanes((8, 128))
    for p in range(2):
        quarter = ((lane8 // 16) % 4 + lane8 // 64 + 2 * p) % 4
        wants = [packed[a][16:24].astype(jnp.int32) - quarter for a in range(8)]
        for t in range(32):
            tile = jnp.zeros((16, 128), F32)
            for a in range(8):
                hit = wants[a] == 4 * t
                hit = jnp.concatenate([hit, hit], axis=0)
                tile = tile + jnp.where(hit, packed[a][0:16], 0.0)
            couple[p, t * 16 : (t + 1) * 16, :] = tile


def spread_kernel(*refs):
    msgs, out, (total, couple) = refs[:4], refs[4], refs[5:]
    fill_couple(msgs, couple, total)
    value = msgs[0][0:32, :]
    for ref in msgs[1:]:
        value = value + ref[0:32, :]
    fwd = value[0:16].astype(BF16)
    bwd = value[16:32]
    lane16 = lanes((16, 128))
    block = jnp.concatenate(
        [jnp.where(lane16 // 32 == g, bwd, 0.0) for g in range(4)], axis=0
    )
    contrib = jnp.zeros((512, 128), F32)
    for p in range(2):
        rhs = jnp.concatenate(
            [block if d == 0 else pltpu.roll(block, 32 * d, 1) for d in (2 * p, 2 * p + 1)],
            axis=0,
        )
        r_hi, r_lo = split(rhs)
        k_hi, k_lo = split(couple[p])
        contrib = contrib + (dot(k_hi, r_lo) + dot(k_lo, r_hi)) + dot(k_hi, r_hi)
    contrib = contrib.astype(BF16)
    for t in range(32):
        out[t, 0:16, :] = fwd
        out[t, 16:32, :] = contrib[t * 16 : (t + 1) * 16]


def collect_kernel(arrived, *refs):
    msgs, outs, (picked, groups, couple) = refs[:4], refs[4:8], refs[8:]
    fill_couple(msgs, couple, groups)
    me = lax.rem(lax.axis_index("curve"), QUAD)
    total = arrived[0, 16:32, :].astype(F32)
    for t in range(1, 32):
        total = total + arrived[t, 16:32, :].astype(F32)
    source = jnp.concatenate([arrived[t, 0:16, :] for t in range(32)], axis=0)
    over_rows = (((0,), (0,)), ((), ()))
    for p in range(2):
        k_hi, k_lo = split(couple[p])
        picked[p * 128 : (p + 1) * 128, :] = dot(k_hi, source, over_rows) + dot(
            k_lo, source, over_rows
        )
    for os in range(4):
        owner = me ^ os
        far = jnp.zeros((16, 128), F32)
        for d in range(4):
            rows = picked[pl.ds(pl.multiple_of(d * 64 + owner * 16, 16), 16), :]
            far = far + moved(rows, me - owner - d, me)
        outs[os][0:16, :] = far.astype(BF16)
        outs[os][16:32, :] = moved(total, me - owner, me).astype(BF16)


def fetch_kernel(near, own, near_v, own_v, sems):
    copies = [
        pltpu.make_async_copy(near, near_v, sems.at[0]),
        pltpu.make_async_copy(own, own_v, sems.at[1]),
    ]
    for copy in copies:
        copy.start()
    for copy in copies:
        copy.wait()


def finish_kernel(
    near, own, arrived, b_in, b_out, m0, m1, m2, m3, layer, grad, layer_v, grad_v, sems
):
    value = ((m0[...] + m1[...]) + (m2[...] + m3[...])).astype(BF16)
    far = value[0:16]
    coarse_t = value[16:32].astype(F32).T.astype(BF16)
    copies = []
    part = near.shape[0] // PARTS
    for n in range(PARTS):
        for i in range(n * part, (n + 1) * part):
            term = dot(b_out[i], far, (((0,), (0,)), ((), ())))
            layer_v[i] = (near[i] + term).astype(BF16)
            total = own[i] + arrived[i].astype(F32) + dot(coarse_t, b_in[i])
            grad_v[i] = total.astype(BF16).T
        for j, (src, dst) in enumerate(((layer_v, layer), (grad_v, grad))):
            rows = pl.ds(n * part, part)
            copies.append(pltpu.make_async_copy(src.at[rows], dst.at[rows], sems.at[n, j]))
            copies[-1].start()
    for copy in copies:
        copy.wait()


def layer_step(
    features,
    cotangent,
    near_kernel,
    near_index,
    near_count,
    basis_in,
    basis_out,
    far_kernel,
    far_index,
    channel_mix,
):
    groups = lax.axis_size("curve")
    blocks = near_kernel.shape[0]
    places = groups // QUAD
    index = near_index.T
    cube = (blocks, 128, 128)

    b_out = jnp.swapaxes(basis_out, 1, 2)
    rows32 = jax.ShapeDtypeStruct((32, 128), F32)
    vmem = pl.BlockSpec(memory_space=pltpu.VMEM)
    smem = pl.BlockSpec(memory_space=pltpu.SMEM)
    raw = pl.BlockSpec(memory_space=pl.ANY)
    keep, give, cot_v = pl.pallas_call(
        project_kernel,
        out_shape=[rows32, rows32, pltpu.VMEM(cube, BF16)],
        in_specs=[raw] * 5,
        out_specs=[vmem] * 3,
        scratch_shapes=[
            pltpu.VMEM(cube, BF16),
            pltpu.VMEM((blocks, 16, 128), BF16),
            pltpu.VMEM((blocks, 16, 128), BF16),
            pltpu.VMEM((256, 256), F32),
            pltpu.SemaphoreType.DMA((PARTS + 1, 4)),
        ],
        compiler_params=params(14, None),
        cost_estimate=pl.CostEstimate(flops=8 << 30, bytes_accessed=3 << 20, transcendentals=0),
        name="project",
    )(
        hbm(features.reshape(cube)),
        hbm(cotangent.reshape(cube)),
        hbm(basis_in),
        hbm(b_out),
        hbm(channel_mix),
    )
    got = lax.ppermute(give, "chan", [(0, 1), (1, 0)])
    halo = lax.ppermute(features, "curve", [(i, i + 1) for i in range(groups - 1)])
    msgs = pl.pallas_call(
        deal_kernel,
        out_shape=[jax.ShapeDtypeStruct((56, 128), F32)] * 4,
        in_specs=[smem, vmem, vmem, vmem],
        compiler_params=params(6, None),
        name="deal",
    )(far_index, far_kernel.reshape(128, 16), keep, got)
    seen = [msgs[0]]
    for o in range(1, 4):
        seen.append(lax.ppermute(msgs[o], "curve", [(i, i ^ o) for i in range(groups)]))

    prev, own = pl.pallas_call(
        backward_kernel,
        out_shape=[jax.ShapeDtypeStruct(cube, BF16), pltpu.HBM(cube, F32)],
        in_specs=[smem, smem, vmem, vmem],
        out_specs=[vmem, raw],
        scratch_shapes=[
            pltpu.VMEM((2 * blocks + 1, 128, 128), F32),
            pltpu.SemaphoreType.DMA((PARTS,)),
        ],
        compiler_params=params(16, None),
        cost_estimate=pl.CostEstimate(flops=8 << 30, bytes_accessed=12 << 20, transcendentals=0),
        name="backward",
    )(index, near_count, near_kernel, cot_v)
    arrived = lax.ppermute(prev, "curve", [(i + 1, i) for i in range(groups - 1)])

    out_msg = pl.pallas_call(
        spread_kernel,
        out_shape=jax.ShapeDtypeStruct((places, 32, 128), BF16),
        scratch_shapes=[
            pltpu.VMEM((4, 24, 128), F32),
            pltpu.VMEM((2, places * 16, 128), F32),
        ],
        compiler_params=params(6, None),
        name="spread",
    )(*seen)
    rings = [[t * QUAD + s for t in range(places)] for s in range(QUAD)]
    in_msg = lax.all_to_all(out_msg, "curve", 0, 0, tiled=True, axis_index_groups=rings)

    near = pl.pallas_call(
        forward_kernel,
        out_shape=pltpu.HBM(cube, F32),
        in_specs=[smem, smem, raw, raw, raw],
        out_specs=raw,
        scratch_shapes=[
            pltpu.VMEM((2 * blocks + 1, 128, 128), BF16),
            pltpu.VMEM(near_kernel.shape, BF16),
            pltpu.VMEM(cube, F32),
            pltpu.SemaphoreType.DMA((CHUNKS,)),
            pltpu.SemaphoreType.DMA((2,)),
            pltpu.SemaphoreType.DMA((CHUNKS,)),
        ],
        compiler_params=params(16, None),
        cost_estimate=pl.CostEstimate(flops=8 << 30, bytes_accessed=12 << 20, transcendentals=0),
        name="forward",
    )(index, near_count, hbm(near_kernel), hbm(halo.reshape(cube)), hbm(features.reshape(cube)))

    back = pl.pallas_call(
        collect_kernel,
        out_shape=[jax.ShapeDtypeStruct((32, 128), BF16)] * 4,
        scratch_shapes=[
            pltpu.VMEM((256, 128), F32),
            pltpu.VMEM((4, 24, 128), F32),
            pltpu.VMEM((2, places * 16, 128), F32),
        ],
        compiler_params=params(6, None),
        name="collect",
    )(in_msg, *seen)
    near_back, own_back = pl.pallas_call(
        fetch_kernel,
        out_shape=[pltpu.VMEM(cube, F32)] * 2,
        in_specs=[raw, raw],
        out_specs=[vmem, vmem],
        scratch_shapes=[pltpu.SemaphoreType.DMA((2,))],
        compiler_params=params(6, None),
        cost_estimate=pl.CostEstimate(flops=1 << 20, bytes_accessed=8 << 20, transcendentals=0),
        name="fetch",
    )(hbm(near), hbm(own))
    home = [back[0]]
    for o in range(1, 4):
        home.append(lax.ppermute(back[o], "curve", [(i, i ^ o) for i in range(groups)]))

    layer, grad = pl.pallas_call(
        finish_kernel,
        out_shape=[pltpu.HBM(cube, BF16)] * 2,
        in_specs=[vmem] * 9,
        out_specs=[raw, raw],
        scratch_shapes=[
            pltpu.VMEM(cube, BF16),
            pltpu.VMEM(cube, BF16),
            pltpu.SemaphoreType.DMA((PARTS, 2)),
        ],
        compiler_params=params(14, None),
        name="finish",
    )(near_back, own_back, arrived, basis_in, b_out, *home)
    return (layer.reshape(features.shape), grad.reshape(features.shape))


def solution(mesh):
    return jax.shard_map(
        layer_step,
        mesh=mesh,
        in_specs=(
            P("curve", "chan"),
            P("curve", "chan"),
            P("curve", None, None, None),
            P("curve", None),
            P("curve"),
            P("curve", None, None),
            P("curve", None, None),
            P("curve", None, None, None),
            P("curve", None),
            P(),
        ),
        out_specs=(P("curve", "chan"), P("curve", "chan")),
        check_vma=False,
    )
```

```python
import jax
import jax.numpy as jnp
from jax import lax
from jax.experimental import pallas as pl
from jax.experimental.pallas import tpu as pltpu
from jax.sharding import PartitionSpec as P


F32 = jnp.float32
BF16 = jnp.bfloat16
MIB = 1 << 20
QUAD = 4
PARTS = 4
UNROLL = 4
CHUNKS = (2, 6, 8, 8, 8)
AHEAD = 3


def params(mib, semantics=("arbitrary",)):
    return pltpu.CompilerParams(dimension_semantics=semantics, vmem_limit_bytes=mib * MIB)


def dot(a, b, dims=(((1,), (0,)), ((), ()))):
    return lax.dot_general(a, b, dims, preferred_element_type=F32)


def split(value):
    high = value.astype(BF16)
    return high, (value - high.astype(F32)).astype(BF16)


def hbm(value):
    return pltpu.with_memory_space_constraint(value, pltpu.HBM)


def lanes(shape):
    return lax.broadcasted_iota(jnp.int32, shape, 1)


def moved(value, block, keep):
    rolled = pltpu.roll(value, lax.rem(block * 32 + 256, 128), 1)
    return jnp.where(lanes(value.shape) // 32 == keep, rolled, 0.0)


def project_kernel(feat, cot, b_in, b_out, mix, keep, give, cot_v, feat_v, b_in_v, b_out_v, mix_v, sems):
    count = feat.shape[0]
    part = count // PARTS
    loads = []
    for n in range(PARTS):
        rows = pl.ds(n * part, part)
        loads.append(
            [
                pltpu.make_async_copy(src.at[rows], dst, sems.at[n, j])
                for j, (src, dst) in enumerate(
                    (
                        (feat, feat_v.at[rows]),
                        (b_in, b_in_v.at[rows]),
                        (cot, cot_v.at[rows]),
                        (b_out, b_out_v.at[rows]),
                    )
                )
            ]
        )
    last = pltpu.make_async_copy(mix, mix_v, sems.at[PARTS, 0])
    for copy in [c for group in loads for c in group] + [last]:
        copy.start()

    acc_f = jnp.zeros((16, 128), F32)
    acc_b = jnp.zeros((16, 128), F32)
    for n in range(PARTS):
        for copy in loads[n]:
            copy.wait()
        picks = range(n * part, (n + 1) * part)
        acc_f += dot(
            jnp.concatenate([b_in_v[i] for i in picks], axis=1),
            feat_v[n * part : (n + 1) * part].reshape(part * 128, 128),
        )
        acc_b += dot(
            jnp.concatenate([b_out_v[i] for i in picks], axis=1),
            cot_v[n * part : (n + 1) * part].reshape(part * 128, 128),
        )
    last.wait()
    half = lax.axis_index("chan")
    start = pl.multiple_of(half * 128, 128)
    exact = lax.Precision.HIGHEST
    coarse = acc_f.astype(BF16).astype(F32)
    for oh, out in enumerate((keep, give)):
        there = pl.multiple_of((half ^ oh) * 128, 128)
        out[0:16, :] = jnp.dot(
            coarse,
            mix_v[pl.ds(start, 128), pl.ds(there, 128)],
            precision=exact,
            preferred_element_type=F32,
        )
        out[16:32, :] = lax.dot_general(
            acc_b,
            mix_v[pl.ds(there, 128), pl.ds(start, 128)],
            (((1,), (1,)), ((), ())),
            precision=exact,
            preferred_element_type=F32,
        )


def deal_kernel(far_index, far, keep, got, *outs):
    me = lax.rem(lax.axis_index("curve"), QUAD)
    both = keep[...] + got[...]
    wide = jnp.concatenate([far[...], jnp.zeros((128, 112), F32)], axis=1)
    pack = wide.T[0:16]
    lane = lanes((8, 128)) // 16
    row = jnp.zeros((8, 128), jnp.int32)
    for a in range(8):
        row = jnp.where(lane == a, far_index[0, a], row)
    for os in range(4):
        outs[os][0:32, :] = moved(both, me - (me ^ os), me)
        outs[os][32:48, :] = pack
        outs[os][48:56, :] = row.astype(F32)


def tile_copies(near, near_v, sems):
    copies = []
    first = 0
    for n, size in enumerate(CHUNKS):
        span = pl.ds(first, size)
        copies.append(pltpu.make_async_copy(near.at[span], near_v.at[span], sems.at[n]))
        first += size
    return copies


def backward_kernel(index, count, near, cot, prev, own, acc, out_sems):
    base = (lax.axis_index("curve") - 1) * 32
    acc[...] = jnp.zeros_like(acc)
    part = near.shape[0] // PARTS
    stores = []
    for n in reversed(range(PARTS)):

        def some(step, carry):
            for i in range(UNROLL):
                b = (n + 1) * part - 1 - (step * UNROLL + i)
                cot_t = cot[b].T
                live = count[b]
                for k in range(0, 8, 2):
                    pair = jnp.concatenate([near[b, k], near[b, k + 1]], axis=1)
                    term = dot(cot_t, pair)
                    for j in range(2):
                        row = jnp.where(k + j < live, index[k + j, b] - base, 64)
                        acc[row] += term[:, j * 128 : (j + 1) * 128]
            return carry

        lax.fori_loop(0, part // UNROLL, some, 0)
        done = acc.at[pl.ds(32 + n * part, part)]
        stores.append(pltpu.make_async_copy(done, own.at[pl.ds(n * part, part)], out_sems.at[n]))
        stores[-1].start()
    prev[...] = acc[0:32].astype(BF16)
    for copy in stores:
        copy.wait()


def forward_kernel(index, count, near, halo, feat, out, rows, near_v, out_v, sems, row_sems, out_sems):
    base = (lax.axis_index("curve") - 1) * 32
    heads = [
        pltpu.make_async_copy(feat, rows.at[pl.ds(32, 32)], row_sems.at[0]),
        pltpu.make_async_copy(halo, rows.at[pl.ds(0, 32)], row_sems.at[1]),
    ]
    copies = tile_copies(near, near_v, sems)
    for copy in heads + copies[:1]:
        copy.start()
    rows[64] = jnp.zeros((128, 128), BF16)
    for copy in heads:
        copy.wait()
    for copy in copies[1:AHEAD]:
        copy.start()
    first = 0
    stores = []
    for n, copy in enumerate(copies):
        copy.wait()
        if n + AHEAD < len(CHUNKS):
            copies[n + AHEAD].start()
        for b in range(first, first + CHUNKS[n]):
            live = count[b]
            picked = [rows[jnp.where(k < live, index[k, b] - base, 64)] for k in range(8)]
            tiles = jnp.concatenate([near_v[b, k] for k in range(8)], axis=1)
            out_v[b] = dot(tiles, jnp.concatenate(picked, axis=0))
        span = pl.ds(first, CHUNKS[n])
        stores.append(pltpu.make_async_copy(out_v.at[span], out.at[span], out_sems.at[n]))
        stores[-1].start()
        first += CHUNKS[n]
    for copy in stores:
        copy.wait()


def fill_couple(msgs, couple, total):
    me = lax.rem(lax.axis_index("curve"), QUAD)
    lane = lanes((24, 128))
    for os in range(4):
        total[me ^ os] = msgs[os][32:56, :]
    packed = []
    for a in range(8):
        group = jnp.zeros((24, 128), F32)
        for g in range(4):
            rolled = pltpu.roll(total[g], (16 * (g - a)) % 128, 1)
            group = jnp.where(lane // 16 == g, rolled, group)
        packed.append(group + pltpu.roll(group, 64, 1))
    lane8 = lanes((8, 128))
    for p in range(2):
        quarter = ((lane8 // 16) % 4 + lane8 // 64 + 2 * p) % 4
        wants = [packed[a][16:24].astype(jnp.int32) - quarter for a in range(8)]
        for t in range(32):
            tile = jnp.zeros((16, 128), F32)
            for a in range(8):
                hit = wants[a] == 4 * t
                hit = jnp.concatenate([hit, hit], axis=0)
                tile = tile + jnp.where(hit, packed[a][0:16], 0.0)
            couple[p, t * 16 : (t + 1) * 16, :] = tile


def spread_kernel(*refs):
    msgs, out, (total, couple, held, sems) = refs[:4], refs[4], refs[5:]
    fill_couple(msgs, couple, total)
    value = msgs[0][0:32, :]
    for ref in msgs[1:]:
        value = value + ref[0:32, :]
    fwd = value[0:16].astype(BF16)
    bwd = value[16:32]
    lane16 = lanes((16, 128))
    block = jnp.concatenate(
        [jnp.where(lane16 // 32 == g, bwd, 0.0) for g in range(4)], axis=0
    )
    sides = []
    for p in range(2):
        rhs = jnp.concatenate(
            [block if d == 0 else pltpu.roll(block, 32 * d, 1) for d in (2 * p, 2 * p + 1)],
            axis=0,
        )
        sides.append(split(rhs))
    copies = []
    for n in range(PARTS):
        contrib = jnp.zeros((128, 128), F32)
        for p in range(2):
            r_hi, r_lo = sides[p]
            k_hi, k_lo = split(couple[p, n * 128 : (n + 1) * 128, :])
            contrib = contrib + (dot(k_hi, r_lo) + dot(k_lo, r_hi)) + dot(k_hi, r_hi)
        contrib = contrib.astype(BF16)
        for i in range(8):
            held[n * 8 + i, 0:16, :] = fwd
            held[n * 8 + i, 16:32, :] = contrib[i * 16 : (i + 1) * 16]
        span = pl.ds(n * 8, 8)
        copies.append(pltpu.make_async_copy(held.at[span], out.at[span], sems.at[n]))
        copies[-1].start()
    for copy in copies:
        copy.wait()


def collect_kernel(arrived, *refs):
    msgs, outs, (picked, groups, couple) = refs[:4], refs[4:8], refs[8:]
    fill_couple(msgs, couple, groups)
    me = lax.rem(lax.axis_index("curve"), QUAD)
    total = arrived[0, 16:32, :].astype(F32)
    for t in range(1, 32):
        total = total + arrived[t, 16:32, :].astype(F32)
    source = jnp.concatenate([arrived[t, 0:16, :] for t in range(32)], axis=0)
    over_rows = (((0,), (0,)), ((), ()))
    for p in range(2):
        k_hi, k_lo = split(couple[p])
        picked[p * 128 : (p + 1) * 128, :] = dot(k_hi, source, over_rows) + dot(
            k_lo, source, over_rows
        )
    for os in range(4):
        owner = me ^ os
        far = jnp.zeros((16, 128), F32)
        for d in range(4):
            rows = picked[pl.ds(pl.multiple_of(d * 64 + owner * 16, 16), 16), :]
            far = far + moved(rows, me - owner - d, me)
        outs[os][0:16, :] = far.astype(BF16)
        outs[os][16:32, :] = moved(total, me - owner, me).astype(BF16)


def fetch_kernel(near, own, near_v, own_v, sems):
    copies = [
        pltpu.make_async_copy(near, near_v, sems.at[0]),
        pltpu.make_async_copy(own, own_v, sems.at[1]),
    ]
    for copy in copies:
        copy.start()
    for copy in copies:
        copy.wait()


def finish_kernel(
    near, own, arrived, b_in, b_out, m0, m1, m2, m3, layer, grad, layer_v, grad_v, sems
):
    value = ((m0[...] + m1[...]) + (m2[...] + m3[...])).astype(BF16)
    far = value[0:16]
    coarse_t = value[16:32].astype(F32).T.astype(BF16)
    copies = []
    part = near.shape[0] // PARTS
    for n in range(PARTS):
        for i in range(n * part, (n + 1) * part):
            term = dot(b_out[i], far, (((0,), (0,)), ((), ())))
            layer_v[i] = (near[i] + term).astype(BF16)
            total = own[i] + arrived[i].astype(F32) + dot(coarse_t, b_in[i])
            grad_v[i] = total.astype(BF16).T
        for j, (src, dst) in enumerate(((layer_v, layer), (grad_v, grad))):
            rows = pl.ds(n * part, part)
            copies.append(pltpu.make_async_copy(src.at[rows], dst.at[rows], sems.at[n, j]))
            copies[-1].start()
    for copy in copies:
        copy.wait()


def layer_step(
    features,
    cotangent,
    near_kernel,
    near_index,
    near_count,
    basis_in,
    basis_out,
    far_kernel,
    far_index,
    channel_mix,
):
    groups = lax.axis_size("curve")
    blocks = near_kernel.shape[0]
    places = groups // QUAD
    index = near_index.T
    cube = (blocks, 128, 128)

    b_out = jnp.swapaxes(basis_out, 1, 2)
    rows32 = jax.ShapeDtypeStruct((32, 128), F32)
    vmem = pl.BlockSpec(memory_space=pltpu.VMEM)
    smem = pl.BlockSpec(memory_space=pltpu.SMEM)
    raw = pl.BlockSpec(memory_space=pl.ANY)
    keep, give, cot_v = pl.pallas_call(
        project_kernel,
        out_shape=[rows32, rows32, pltpu.VMEM(cube, BF16)],
        in_specs=[raw] * 5,
        out_specs=[vmem] * 3,
        scratch_shapes=[
            pltpu.VMEM(cube, BF16),
            pltpu.VMEM((blocks, 16, 128), BF16),
            pltpu.VMEM((blocks, 16, 128), BF16),
            pltpu.VMEM((256, 256), F32),
            pltpu.SemaphoreType.DMA((PARTS + 1, 4)),
        ],
        compiler_params=params(14, None),
        cost_estimate=pl.CostEstimate(flops=8 << 30, bytes_accessed=3 << 20, transcendentals=0),
        name="project",
    )(
        hbm(features.reshape(cube)),
        hbm(cotangent.reshape(cube)),
        hbm(basis_in),
        hbm(b_out),
        hbm(channel_mix),
    )
    got = lax.ppermute(give, "chan", [(0, 1), (1, 0)])
    halo = lax.ppermute(features, "curve", [(i, i + 1) for i in range(groups - 1)])
    msgs = pl.pallas_call(
        deal_kernel,
        out_shape=[jax.ShapeDtypeStruct((56, 128), F32)] * 4,
        in_specs=[smem, vmem, vmem, vmem],
        compiler_params=params(6, None),
        name="deal",
    )(far_index, far_kernel.reshape(128, 16), keep, got)
    seen = [msgs[0]]
    for o in range(1, 4):
        seen.append(lax.ppermute(msgs[o], "curve", [(i, i ^ o) for i in range(groups)]))

    prev, own = pl.pallas_call(
        backward_kernel,
        out_shape=[jax.ShapeDtypeStruct(cube, BF16), pltpu.HBM(cube, F32)],
        in_specs=[smem, smem, vmem, vmem],
        out_specs=[vmem, raw],
        scratch_shapes=[
            pltpu.VMEM((2 * blocks + 1, 128, 128), F32),
            pltpu.SemaphoreType.DMA((PARTS,)),
        ],
        compiler_params=params(16, None),
        cost_estimate=pl.CostEstimate(flops=8 << 30, bytes_accessed=12 << 20, transcendentals=0),
        name="backward",
    )(index, near_count, near_kernel, cot_v)
    arrived = lax.ppermute(prev, "curve", [(i + 1, i) for i in range(groups - 1)])

    out_msg = pl.pallas_call(
        spread_kernel,
        out_shape=pltpu.HBM((places, 32, 128), BF16),
        out_specs=raw,
        scratch_shapes=[
            pltpu.VMEM((4, 24, 128), F32),
            pltpu.VMEM((2, places * 16, 128), F32),
            pltpu.VMEM((places, 32, 128), BF16),
            pltpu.SemaphoreType.DMA((PARTS,)),
        ],
        compiler_params=params(6, None),
        name="spread",
    )(*seen)
    rings = [[t * QUAD + s for t in range(places)] for s in range(QUAD)]
    in_msg = lax.all_to_all(out_msg, "curve", 0, 0, tiled=True, axis_index_groups=rings)

    near = pl.pallas_call(
        forward_kernel,
        out_shape=pltpu.HBM(cube, F32),
        in_specs=[smem, smem, raw, raw, raw],
        out_specs=raw,
        scratch_shapes=[
            pltpu.VMEM((2 * blocks + 1, 128, 128), BF16),
            pltpu.VMEM(near_kernel.shape, BF16),
            pltpu.VMEM(cube, F32),
            pltpu.SemaphoreType.DMA((len(CHUNKS),)),
            pltpu.SemaphoreType.DMA((2,)),
            pltpu.SemaphoreType.DMA((len(CHUNKS),)),
        ],
        compiler_params=params(16, None),
        cost_estimate=pl.CostEstimate(flops=8 << 30, bytes_accessed=12 << 20, transcendentals=0),
        name="forward",
    )(index, near_count, hbm(near_kernel), hbm(halo.reshape(cube)), hbm(features.reshape(cube)))

    back = pl.pallas_call(
        collect_kernel,
        out_shape=[jax.ShapeDtypeStruct((32, 128), BF16)] * 4,
        scratch_shapes=[
            pltpu.VMEM((256, 128), F32),
            pltpu.VMEM((4, 24, 128), F32),
            pltpu.VMEM((2, places * 16, 128), F32),
        ],
        compiler_params=params(6, None),
        name="collect",
    )(in_msg, *seen)
    near_back, own_back = pl.pallas_call(
        fetch_kernel,
        out_shape=[pltpu.VMEM(cube, F32)] * 2,
        in_specs=[raw, raw],
        out_specs=[vmem, vmem],
        scratch_shapes=[pltpu.SemaphoreType.DMA((2,))],
        compiler_params=params(6, None),
        cost_estimate=pl.CostEstimate(flops=1 << 20, bytes_accessed=8 << 20, transcendentals=0),
        name="fetch",
    )(hbm(near), hbm(own))
    home = [back[0]]
    for o in range(1, 4):
        home.append(lax.ppermute(back[o], "curve", [(i, i ^ o) for i in range(groups)]))

    layer, grad = pl.pallas_call(
        finish_kernel,
        out_shape=[pltpu.HBM(cube, BF16)] * 2,
        in_specs=[vmem] * 9,
        out_specs=[raw, raw],
        scratch_shapes=[
            pltpu.VMEM(cube, BF16),
            pltpu.VMEM(cube, BF16),
            pltpu.SemaphoreType.DMA((PARTS, 2)),
        ],
        compiler_params=params(14, None),
        name="finish",
    )(near_back, own_back, arrived, basis_in, b_out, *home)
    return (layer.reshape(features.shape), grad.reshape(features.shape))


def solution(mesh):
    return jax.shard_map(
        layer_step,
        mesh=mesh,
        in_specs=(
            P("curve", "chan"),
            P("curve", "chan"),
            P("curve", None, None, None),
            P("curve", None),
            P("curve"),
            P("curve", None, None),
            P("curve", None, None),
            P("curve", None, None, None),
            P("curve", None),
            P(),
        ),
        out_specs=(P("curve", "chan"), P("curve", "chan")),
        check_vma=False,
    )
```
